256 devices in a mesh: seq: 32 (over x, z), head: 8 (over y, core).
Axes of the slice: x: 4, y: 4, z: 8, core: 2. Of those that a mesh axis runs over, the one named last changes fastest.
Arguments:
- tokens: bfloat16 [8192, 3072], P('seq', 'head'), may hold values from -6 to 6
- norm_gain: float32 [3072], replicated, may hold values from 0.1 to 1.9
- w_query: bfloat16 [3072, 3072], P(None, 'head'), may hold values from -0.109375 to 0.109375
- w_key: bfloat16 [3072, 1024], P(None, 'head'), may hold values from -0.3125 to 0.3125
- w_value: bfloat16 [3072, 1024], P(None, 'head'), may hold values from -0.109375 to 0.109375
- w_out: bfloat16 [3072, 3072], P('head'), may hold values from -0.109375 to 0.109375
- keys_cache: bfloat16 [65536, 1024], P('seq', 'head'), may hold values from -120 to 120
- values_cache: bfloat16 [65536, 1024], P('seq', 'head'), may hold values from -6 to 6
- cached_lengths: int32 [4], replicated, may hold values from 0 to 14336, as said below
- rope_offsets: int32 [4], replicated, may hold values from 0 to 8191
Outputs:
- attn_proj: bfloat16 [8192, 3072], P('seq', 'head')
- keys_updated: bfloat16 [65536, 1024], P('seq', 'head')
- values_updated: bfloat16 [65536, 1024], P('seq', 'head')
The draws below stay inside these ranges and needn't reach their ends.
Inputs may be any that keep to these rules, and one draw needn't show every extreme that they name: `cached_lengths`: in every draw one request has exactly 14336 cached tokens.
All inputs are finite; a program needn't handle non-finite values.
Results may differ from the reference program's by a relative error of at most 0.02.
Values may be sent and summed in bfloat16 or wider, within the bound.
A program may use at most 128 MiB of HBM per device.

```python
import math
import jax
import jax.numpy as jnp
from jax import lax

D = 3072
HQ = 24
KV = 8
HD = 128
TOK_DEV = 256
REQS = 4
GROUP = 8
NEW_LEN = 2048
CACHE_MAX = 14336
CAP_DEV = 2048
TOKENS = 8192
SLOTS = 65536


def draw_keys_cache(key, part):
    first_key = jax.random.fold_in(key, 0)
    entries = jnp.clip(jax.random.normal(first_key, (SLOTS, KV * HD), jnp.float32), -3.3, 3.3) * 3.0
    return entries.astype(jnp.bfloat16)


def draw_values_cache(key, part):
    first_key, second_key = jax.random.split(key)
    noise = jnp.clip(jax.random.normal(first_key, (SLOTS // CAP_DEV, CAP_DEV, KV * HD), jnp.float32), -4.0, 4.0)
    offsets = jax.random.uniform(second_key, (SLOTS // CAP_DEV, 1, KV * HD), jnp.float32, -2.0, 2.0)
    shifted = noise + offsets
    return shifted.reshape(SLOTS, KV * HD).astype(jnp.bfloat16)


def draw_cached_lengths(key, part):
    first_key, second_key = jax.random.split(key)
    lengths = jax.random.randint(first_key, (REQS,), 0, CACHE_MAX + 1)
    longest = jax.random.randint(second_key, (), 0, REQS)
    return jnp.where(jnp.arange(REQS) == longest, CACHE_MAX, lengths).astype(jnp.int32)


def plant(values, stream_key, smallest, top_value):
    extent = values.shape
    place = [jax.random.randint(jax.random.fold_in(stream_key, axis), (), 0, extent[axis]) for axis in range(len(extent))]
    values = values.at[tuple(place)].set(smallest)
    longest = extent.index(max(extent))
    place[longest] = (place[longest] + 1) % extent[longest]
    return values.at[tuple(place)].set(top_value)


def shard_levels(own_key, shape, cuts, low, high):
    def one(axis_at, parts):
        draws = jax.random.uniform(jax.random.fold_in(jax.random.fold_in(own_key, 6), axis_at), (parts,), jnp.float32, low / len(cuts), high / len(cuts))
        return jnp.repeat(jnp.exp(draws), shape[axis_at] // parts).reshape((-1,) + (1,) * (len(shape) - axis_at - 1))

    gain = one(*cuts[0])
    for cut in cuts[1:]:
        gain = gain * one(*cut)
    return gain


def scatter_about(rng, dims, spread, most, cuts=(), held_as=jnp.bfloat16):
    level = shard_levels(rng, dims, cuts, -0.22, 0.18) if cuts else 1.0
    values = jax.random.normal(rng, dims, jnp.float32) * spread * level
    return jnp.minimum(jnp.maximum(values, -most), most).astype(held_as)


def setup_inputs(seed: int = 0) -> dict:
    key_list = jax.random.split(jax.random.key(seed), 11)
    tokens = scatter_about(key_list[0], (TOKENS, D), 1.0, 6.0, ((0, 32), (1, 8)))
    norm_gain = jnp.clip(1.0 + 0.18 * jax.random.normal(key_list[1], (D,), jnp.float32), 0.1, 1.9)
    w_query = scatter_about(key_list[2], (D, HQ * HD), D ** -0.5, 0.109375, ((1, 8),))
    w_key = scatter_about(key_list[3], (D, KV * HD), (D // 9) ** -0.5, 0.3125, ((1, 8),))
    w_value = scatter_about(key_list[4], (D, KV * HD), D ** -0.5, 0.109375, ((1, 8),))
    w_out = scatter_about(key_list[5], (HQ * HD, D), (HQ * HD) ** -0.5, 0.109375, ((0, 8),))
    keys_cache = draw_keys_cache(jax.random.fold_in(key_list[10], 71), 0)
    values_cache = draw_values_cache(jax.random.fold_in(key_list[10], 71), 0)
    cached_lengths = draw_cached_lengths(jax.random.fold_in(key_list[10], 71), 0)
    rope_offsets = plant(jax.random.randint(key_list[9], (REQS,), 0, 8192), jax.random.fold_in(key_list[9], 1), 0, 8191).astype(jnp.int32)
    return {"tokens": tokens, "norm_gain": norm_gain, "w_query": w_query, "w_key": w_key, "w_value": w_value, "w_out": w_out, "keys_cache": keys_cache, "values_cache": values_cache, "cached_lengths": cached_lengths, "rope_offsets": rope_offsets}


rope_base = 500000.0

def rotate(vectors, positions):
    half_width = vectors.shape[-1] // 2
    frequency = rope_base ** (-jnp.arange(half_width, dtype=jnp.float32) * 2.0 / vectors.shape[-1])
    angles = positions.astype(jnp.float32)[:, None] * frequency[None, :]
    cosine = jnp.cos(angles)[:, None, :]
    sine_part = jnp.sin(angles)[:, None, :]
    first_half = vectors[..., :half_width]
    second_half = vectors[..., half_width:]
    return jnp.concatenate([first_half * cosine - second_half * sine_part, second_half * cosine + first_half * sine_part], -1)

def to_requests(array, rows):
    width = array.shape[-1]
    return array.reshape(GROUP, REQS, rows, width).transpose(1, 0, 2, 3).reshape(REQS * GROUP * rows, width)

def from_requests(array, rows):
    width = array.shape[-1]
    return array.reshape(REQS, GROUP, rows, width).transpose(1, 0, 2, 3).reshape(REQS * GROUP * rows, width)

def reference(tokens, norm_gain, w_query, w_key, w_value, w_out, keys_cache, values_cache, cached_lengths, rope_offsets):
    ordered = to_requests(tokens, TOK_DEV)
    widened = ordered.astype(jnp.float32)
    normed = (widened * lax.rsqrt(lax.optimization_barrier(jnp.mean(widened * widened, -1, keepdims=True)) + 1e-05) * norm_gain).astype(jnp.bfloat16)
    token_index = jnp.arange(TOKENS, dtype=jnp.int32)
    owner = token_index // NEW_LEN
    within = token_index % NEW_LEN
    positions = rope_offsets[owner] + cached_lengths[owner] + within
    repeat = HQ // KV
    queries = rotate(jnp.dot(normed, w_query, preferred_element_type=jnp.float32).reshape(TOKENS, HQ, HD), positions).astype(jnp.bfloat16)
    new_keys = rotate(jnp.dot(normed, w_key, preferred_element_type=jnp.float32).reshape(TOKENS, KV, HD), positions).astype(jnp.bfloat16)
    new_values = jnp.dot(normed, w_value, preferred_element_type=jnp.float32).astype(jnp.bfloat16)
    capacity = SLOTS // REQS
    slots = jnp.arange(capacity, dtype=jnp.int32)
    source = slots[None, :] - cached_lengths[:, None]
    inside = (source >= 0) & (source < NEW_LEN)
    picked = jnp.clip(source, 0, NEW_LEN - 1).astype(jnp.int32)

    def update(old_cache, fresh):
        old_cache = to_requests(old_cache, CAP_DEV).reshape(REQS, capacity, KV * HD)
        fresh = fresh.reshape(REQS, NEW_LEN, KV * HD)
        chosen = jnp.take_along_axis(fresh, picked[:, :, None], axis=1)
        return jnp.where(inside[:, :, None], chosen, old_cache).reshape(SLOTS, KV * HD)
    keys_ordered = update(keys_cache, new_keys)
    values_ordered = update(values_cache, new_values)
    query_rows = math.gcd(NEW_LEN, 128)
    per_request = NEW_LEN // query_rows
    request_ids = (jnp.arange(REQS * per_request, dtype=jnp.int32) // per_request).astype(jnp.int32)
    starts = (jnp.arange(REQS * per_request, dtype=jnp.int32) % per_request * query_rows).astype(jnp.int32)
    key_table = keys_ordered.reshape(REQS, capacity, KV, HD)
    value_table = values_ordered.reshape(REQS, capacity, KV, HD)

    def one_block(block_item):
        request, start = block_item
        query_block = lax.dynamic_slice_in_dim(queries, request * NEW_LEN + start, query_rows, 0)
        query_block = query_block.reshape(query_rows, KV, repeat, HD).astype(jnp.float32)
        key_block = lax.dynamic_index_in_dim(key_table, request, 0, False).astype(jnp.float32)
        value_block = lax.dynamic_index_in_dim(value_table, request, 0, False).astype(jnp.float32)
        scores = jnp.einsum('qgrd,kgd->grqk', query_block, key_block) / math.sqrt(HD)
        limit = lax.dynamic_index_in_dim(cached_lengths, request, 0, False) + start + jnp.arange(query_rows, dtype=jnp.int32)
        visible = slots[None, :] <= limit[:, None]
        masked = jnp.where(visible, scores, -jnp.inf)
        running_max = lax.optimization_barrier(jnp.max(masked, -1, keepdims=True))
        weights = jnp.where(visible, jnp.exp(masked - running_max), 0.0)
        denominator = lax.optimization_barrier(jnp.sum(weights, -1))
        rounded = lax.optimization_barrier(weights.astype(jnp.bfloat16))
        summed = jnp.einsum('grqk,kgd->qgrd', rounded.astype(jnp.float32), value_block)
        return (summed / denominator.transpose(2, 0, 1)[..., None]).astype(jnp.bfloat16)
    attended = lax.map(one_block, (request_ids, starts)).reshape(TOKENS, HQ * HD)
    projected = jnp.dot(attended, w_out, preferred_element_type=jnp.float32).astype(jnp.bfloat16)
    attn_proj = from_requests(projected, TOK_DEV)
    keys_updated = from_requests(keys_ordered, CAP_DEV)
    values_updated = from_requests(values_ordered, CAP_DEV)
    return (attn_proj, keys_updated, values_updated)
```

```python
import math

import jax
import jax.numpy as jnp
from jax import lax
from jax.experimental import pallas as pl
from jax.experimental.pallas import tpu as pltpu
from jax.sharding import PartitionSpec as P

HD = 128
NX = 4
NZ = 8
NY = 4
GROUP = 8
NEG = -(2.0**100)
ROPE_BASE = 500000.0
EPS = 1e-05
LOG2E = 1.4426950408889634
F32 = jnp.float32
BF16 = jnp.bfloat16


def digit(number, place):
    value = number
    result = value % 10
    for at in range(1, 8):
        value = value // 10
        flag = (place + 8 - at) // 8 - (place + 7 - at) // 8
        result = result + flag * (value % 10 - number % 10)
    return result


def order_code(digits):
    return sum(d * 10**i for i, d in enumerate(digits))


ORDER = [(0, 0), (0, 1), (0, 3), (1, 0), (0, 2), (1, 1), (1, 3), (1, 2)]
STEP_FORWARD_Q = ORDER.index((1, 0))
STEP_SEND_KV = 1
STEP_FORWARD_KV = 6


def kernel(
    tok, gain, wq, wk, wv, wo, kc, vc, lens, cos, sin,
    out, kv_out,
    x_all, wq_v, wk_v, wv_v, wo_all, kraw, kT, va, kfT, vfa, acc, ssq,
    q_all, kv_all, o_buf, l_buf, o_in, l_in, oz_out, lz_out, oz_in, lz_in,
    att_all, pr_out, pr_in,
    load_sem, own_wo_sem, ag_send, ag_recv, wo_send, wo_recv, q_send, q_recv, kv_send, kv_recv,
    o_send, o_recv, l_send, l_recv, z_send, z_recv, att_send, att_recv, pr_send, pr_recv, out_sem,
):
    rows, width = tok.shape
    heads = width // HD
    slots = kc.shape[0]
    s = lax.axis_index("seq")
    h = lax.axis_index("head")
    x, z = s // NZ, s % NZ
    zhi = z // 4
    request = s % 4
    y, c = h // 2, h % 2
    p = s // 4
    z_peer = x * NZ + (z + 4) % NZ
    pz = z_peer // 4
    sib = y * 2 + (1 - c)

    def x_peer(d):
        return ((x + d) % NX) * NZ + z

    def y_peer(d):
        return ((y + d) % NY) * 2 + c

    def remote(src, dst, send, recv, seq, head):
        return pltpu.make_async_remote_copy(
            src_ref=src, dst_ref=dst, send_sem=send, recv_sem=recv,
            device_id=(seq, head), device_id_type=pl.DeviceIdType.MESH,
        )

    loads = [
        pltpu.make_async_copy(tok, x_all.at[h], load_sem.at[0]),
        pltpu.make_async_copy(wq, wq_v, load_sem.at[1]),
        pltpu.make_async_copy(wk, wk_v, load_sem.at[2]),
        pltpu.make_async_copy(wv, wv_v, load_sem.at[3]),
        pltpu.make_async_copy(kc, kraw, load_sem.at[4]),
        pltpu.make_async_copy(vc, va.at[:, pl.ds(0, HD)], load_sem.at[5]),
    ]
    for load in loads:
        load.start()

    def wo_columns(yy, cc):
        return wo.at[:, pl.ds(pl.multiple_of((yy * 2 + cc) * width, width), width)]

    def wo_rows(yy, cc):
        return wo_all.at[yy, pl.ds(pl.multiple_of(cc * width, width), width), :]

    own_wo = [
        pltpu.make_async_copy(wo_columns(yy, c), wo_rows(yy, c), own_wo_sem.at[yy])
        for yy in range(NY)
    ]
    for load in own_wo:
        load.start()

    barrier = pltpu.get_barrier_semaphore()
    peers = [(s, sib), (z_peer, h)]
    peers += [(s, y_peer(d)) for d in (1, 2, 3)] + [(x_peer(d), h) for d in (1, 2, 3)]
    for seq, head in peers:
        pl.semaphore_signal(
            barrier, inc=1, device_id=(seq, head), device_id_type=pl.DeviceIdType.MESH
        )
    pl.semaphore_wait(barrier, len(peers))

    def ag_copy(k, source, seq, head, src=None):
        return remote(
            x_all.at[source] if src is None else src, x_all.at[source],
            ag_send.at[k], ag_recv.at[source], seq, head,
        )

    for k, d in enumerate((2, 1, 3)):
        ag_copy(k, h, s, y_peer(d), tok).start()
    ag_copy(3, h, s, sib, tok).start()
    wo_copies = [
        remote(wo_columns(yy, 1 - c), wo_rows(yy, c), wo_send.at[yy], wo_recv.at[yy], s, sib)
        for yy in range(NY)
    ]
    for copy in wo_copies:
        copy.start()

    length = lens[request]
    loads[4].wait()
    loads[5].wait()
    for at in range(0, slots, 512):
        kT[pl.ds(0, HD), pl.ds(at, 512)] = kraw[pl.ds(at, 512), :].T
    slot = p * slots + lax.broadcasted_iota(jnp.int32, (HD, slots), 1)
    first_row = lax.broadcasted_iota(jnp.int32, (HD, slots), 0) == 0
    hidden = jnp.logical_and(first_row, slot >= length)
    kT[pl.ds(HD, HD), :] = jnp.where(hidden, NEG, 0.0).astype(BF16)
    va[:, pl.ds(HD, HD)] = jnp.ones((slots, HD), BF16)
    vfa[:, pl.ds(HD, HD)] = jnp.ones((rows, HD), BF16)
    acc[...] = jnp.zeros_like(acc)
    ssq[...] = jnp.zeros_like(ssq)

    for at in range(4):
        loads[at].wait()

    def project(step, unused):
        d = digit(order_code([0, 0, 1, 3, 2, 1, 3, 2]), step)
        other = digit(order_code([0, 1, 0, 0, 0, 1, 1, 1]), step)
        source = ((y + d) % NY) * 2 + (c + other) % 2

        @pl.when(step > 0)
        def _():
            ag_copy(0, source, s, sib).wait_recv()

        @pl.when(jnp.logical_and(step >= 2, step < 5))
        def _():
            ag_copy(2 + step, source, s, sib).start()

        shard = x_all[source].astype(F32)
        square = shard * shard
        ssq[...] += square[:, :HD] + square[:, HD:2 * HD] + square[:, 2 * HD:]
        scaled = (shard * gain[source]).astype(BF16)
        at = pl.ds(pl.multiple_of(source * width, width), width)
        acc[:, pl.ds(0, width)] += jnp.dot(scaled, wq_v[at, :], preferred_element_type=F32)
        acc[:, pl.ds(width, HD)] += jnp.dot(scaled, wk_v[at, :], preferred_element_type=F32)
        acc[:, pl.ds(width + HD, HD)] += jnp.dot(scaled, wv_v[at, :], preferred_element_type=F32)
        return unused

    lax.fori_loop(0, 8, project, 0)

    scale = lax.rsqrt(jnp.sum(ssq[...], -1, keepdims=True) * (1.0 / (width * 8)) + EPS)
    cosine = cos[...]
    sine = sin[...]

    def rope(vectors):
        return vectors * cosine + pltpu.roll(vectors, HD // 2, 1) * sine

    fold = LOG2E / math.sqrt(HD)
    for hd in range(heads):
        rotated = rope(acc[:, pl.ds(hd * HD, HD)] * scale) * fold
        q_all[p, pl.ds(hd * rows, rows), :] = rotated.astype(BF16)

    def q_copy(k, block, seq):
        return remote(
            q_all.at[block], q_all.at[block], q_send.at[k], q_recv.at[block], seq, h
        )

    def kv_copy(k, block, seq):
        return remote(
            kv_all.at[:, block], kv_all.at[:, block], kv_send.at[k], kv_recv.at[block], seq, h
        )

    q_copy(0, p, z_peer).start()
    for k, d in enumerate((1, 3, 2)):
        q_copy(1 + k, p, x_peer(d)).start()

    fresh_key = rope(acc[:, pl.ds(width, HD)] * scale).astype(BF16)
    fresh_value = (acc[:, pl.ds(width + HD, HD)] * scale).astype(BF16)
    kv_all[0, p] = fresh_key
    kv_all[1, p] = fresh_value
    kfT[...] = fresh_key.T
    vfa[:, pl.ds(0, HD)] = fresh_value

    eye = lax.broadcasted_iota(jnp.int32, (HD, HD), 0) == lax.broadcasted_iota(
        jnp.int32, (HD, HD), 1
    )
    first_lane = lax.broadcasted_iota(jnp.int32, (rows, HD), 1) == 0
    one_lane = jnp.where(first_lane, 1.0, 0.0).astype(BF16)
    offset = lax.broadcasted_iota(jnp.int32, (rows, rows), 0) - lax.broadcasted_iota(
        jnp.int32, (rows, rows), 1
    )

    def o_copies(dz, dx):
        back = (NX - dx) % NX
        return (
            remote(o_buf.at[dz, dx], o_in.at[dz, back], o_send.at[dz, dx], o_recv.at[dz, back],
                   x_peer(dx), h),
            remote(l_buf.at[dz, dx], l_in.at[dz, back], l_send.at[dz, dx], l_recv.at[dz, back],
                   x_peer(dx), h),
        )

    def attend(step, unused):
        dz = digit(order_code([o[0] for o in ORDER]), step)
        dx = digit(order_code([o[1] for o in ORDER]), step)
        block = 2 * ((x + dx) % NX) + (zhi + dz) % 2

        @pl.when(dx + dz > 0)
        def _():
            q_copy(0, block, z_peer).wait_recv()

        @pl.when(step == STEP_FORWARD_Q)
        def _():
            for k, d in enumerate((1, 3, 2)):
                q_copy(4 + k, pz, x_peer(d)).start()

        @pl.when(step == STEP_SEND_KV)
        def _():
            kv_copy(0, p, z_peer).start()
            for k, d in enumerate((1, 3, 2)):
                kv_copy(1 + k, p, x_peer(d)).start()

        @pl.when(step == STEP_FORWARD_KV)
        def _():
            kv_copy(0, pz, z_peer).wait_recv()
            for k, d in enumerate((1, 3, 2)):
                kv_copy(4 + k, pz, x_peer(d)).start()

        def one_head(hd, inner):
            at = pl.ds(pl.multiple_of(hd * rows, rows), rows)
            query = q_all[block, at, :]
            cached = jnp.dot(
                jnp.concatenate([query, one_lane], 1), kT[...], preferred_element_type=F32
            )
            fresh = jnp.dot(query, kfT[...], preferred_element_type=F32)
            fresh = jnp.where(offset + (block - p) * rows >= 0, fresh, NEG)
            top = jnp.maximum(
                jnp.max(cached, -1, keepdims=True), jnp.max(fresh, -1, keepdims=True)
            )
            cached_weights = jnp.exp2(cached - top).astype(BF16)
            fresh_weights = jnp.exp2(fresh - top).astype(BF16)
            summed = jnp.dot(cached_weights, va[...], preferred_element_type=F32)
            summed += jnp.dot(fresh_weights, vfa[...], preferred_element_type=F32)
            total = summed[:, HD:]
            o_buf[dz, dx, at, :] = (summed[:, :HD] / total).astype(BF16)
            logsum = top + jnp.log(total) * LOG2E
            for half in range(rows // HD):
                part = logsum[half * HD:(half + 1) * HD, :]
                l_buf[dz, dx, hd, pl.ds(half, 1), :] = jnp.sum(
                    jnp.where(eye, part, 0.0), 0, keepdims=True
                )
            return inner

        lax.fori_loop(0, heads, one_head, 0)

        @pl.when(dx > 0)
        def _():
            for copy in o_copies(dz, dx):
                copy.start()

        return unused

    l_buf[...] = jnp.zeros_like(l_buf)
    lax.fori_loop(0, GROUP, attend, 0)

    def weigh(logsums):
        highest = logsums[0]
        for one in logsums[1:]:
            highest = jnp.maximum(highest, one)
        shares = [jnp.exp2(one - highest) for one in logsums]
        total = shares[0]
        for one in shares[1:]:
            total = total + one
        return [one / total for one in shares], highest + jnp.log(total) * LOG2E

    def blend(parts, shares, hd, half):
        result = None
        for part, share in zip(parts, shares):
            lanes = share[hd, half:half + 1, :]
            column = jnp.sum(jnp.where(eye, lanes, 0.0), 1, keepdims=True)
            window = pl.ds(hd * rows + half * HD, HD)
            term = part[window, :].astype(F32) * column
            result = term if result is None else result + term
        return result

    def contributions(dz):
        for j in (1, 3, 2):
            for copy in o_copies(dz, (NX - j) % NX):
                copy.wait_recv()
        parts = [o_buf.at[dz, 0]] + [o_in.at[dz, j] for j in (1, 2, 3)]
        logsums = [l_buf[dz, 0]] + [l_in[dz, j] for j in (1, 2, 3)]
        return parts, logsums

    z_copies = (
        remote(oz_out, oz_in, z_send.at[0], z_recv.at[0], z_peer, h),
        remote(lz_out, lz_in, z_send.at[1], z_recv.at[1], z_peer, h),
    )
    parts, logsums = contributions(1)
    shares, merged = weigh(logsums)
    lz_out[...] = merged
    for hd in range(heads):
        for half in range(rows // HD):
            oz_out[pl.ds(hd * rows + half * HD, HD), :] = blend(parts, shares, hd, half).astype(BF16)
    for copy in z_copies:
        copy.start()

    for d in (1, 2, 3):
        kv_copy(0, 2 * ((x + d) % NX) + zhi, z_peer).wait_recv()
        kv_copy(0, 2 * ((x + d) % NX) + (zhi + 1) % 2, z_peer).wait_recv()
    kv_store = pltpu.make_async_copy(kv_all, kv_out.at[:, pl.ds(GROUP, GROUP)], out_sem)
    kv_store.start()

    parts, logsums = contributions(0)
    for copy in z_copies:
        copy.wait_recv()
    shares, merged = weigh(logsums + [lz_in[...]])
    for hd in range(heads):
        for half in range(rows // HD):
            att_all[c, pl.ds(half * HD, HD), pl.ds(hd * HD, HD)] = blend(
                parts + [oz_in], shares, hd, half
            ).astype(BF16)
    att_copy = remote(att_all.at[c], att_all.at[c], att_send, att_recv, s, sib)
    att_copy.start()
    for load in own_wo:
        load.wait()
    for copy in wo_copies:
        copy.wait_recv()
    remote(att_all.at[1 - c], att_all.at[1 - c], att_send, att_recv, s, sib).wait_recv()
    both = jnp.concatenate([att_all[0], att_all[1]], 1)

    def pr_copy(d):
        return remote(
            pr_out.at[d], pr_in.at[(NY - d) % NY], pr_send.at[d], pr_recv.at[(NY - d) % NY],
            s, y_peer(d),
        )

    for d in (2, 1, 3):
        part = jnp.dot(both, wo_all[(y + d) % NY], preferred_element_type=F32)
        pr_out[d] = part.astype(BF16)
        pr_copy(d).start()
    result = jnp.dot(both, wo_all[y], preferred_element_type=F32)
    for j in (1, 3, 2):
        pr_copy((NY - j) % NY).wait_recv()
    for j in (1, 2, 3):
        result = result + pr_in[j].astype(F32)
    out[...] = result.astype(BF16)

    for k in range(3):
        ag_copy(k, h, s, sib, tok).wait_send()
    ag_copy(3, h, s, sib, tok).wait_send()
    for k in range(4, 7):
        ag_copy(k, h, s, sib).wait_send()
    for copy in wo_copies:
        copy.wait_send()
    for k in range(7):
        q_copy(k, p, z_peer).wait_send()
        kv_copy(k, p, z_peer).wait_send()
    for dz in range(2):
        for dx in (1, 2, 3):
            for copy in o_copies(dz, dx):
                copy.wait_send()
    for copy in z_copies:
        copy.wait_send()
    att_copy.wait_send()
    for d in (1, 2, 3):
        pr_copy(d).wait_send()
    kv_store.wait()


def shards(
    tokens, norm_gain, w_query, w_key, w_value, w_out, keys_cache, values_cache,
    cached_lengths, rope_offsets,
):
    rows, width = tokens.shape
    slots = keys_cache.shape[0]
    heads = width // HD
    member = lax.axis_index("seq")
    request = member % 4
    place = member // 4
    length = lax.dynamic_index_in_dim(cached_lengths, request, 0, False)
    offset = lax.dynamic_index_in_dim(rope_offsets, request, 0, False)
    positions = offset + length + place * rows + jnp.arange(rows, dtype=jnp.int32)
    frequency = ROPE_BASE ** (-jnp.arange(HD // 2, dtype=F32) * 2.0 / HD)
    angles = positions.astype(F32)[:, None] * frequency[None, :]
    cosine = jnp.cos(angles)
    sine = jnp.sin(angles)
    cosine = jnp.concatenate([cosine, cosine], 1)
    sine = jnp.concatenate([-sine, sine], 1)

    any_spec = pl.BlockSpec(memory_space=pl.ANY)
    vmem_spec = pl.BlockSpec(memory_space=pltpu.VMEM)
    smem_spec = pl.BlockSpec(memory_space=pltpu.SMEM)
    dma = pltpu.SemaphoreType.DMA
    block = (heads * rows, HD)
    projected, fresh = pl.pallas_call(
        kernel,
        out_shape=(
            jax.ShapeDtypeStruct((rows, width), BF16),
            jax.ShapeDtypeStruct((2, 3 * GROUP, rows, HD), BF16),
        ),
        in_specs=[any_spec, vmem_spec] + [any_spec] * 6 + [smem_spec, vmem_spec, vmem_spec],
        out_specs=(vmem_spec, any_spec),
        scratch_shapes=[
            pltpu.VMEM((8, rows, width), BF16),
            pltpu.VMEM(w_query.shape, BF16),
            pltpu.VMEM(w_key.shape, BF16),
            pltpu.VMEM(w_value.shape, BF16),
            pltpu.VMEM((NY, 2 * width, width), BF16),
            pltpu.VMEM((slots, HD), BF16),
            pltpu.VMEM((2 * HD, slots), BF16),
            pltpu.VMEM((slots, 2 * HD), BF16),
            pltpu.VMEM((HD, rows), BF16),
            pltpu.VMEM((rows, 2 * HD), BF16),
            pltpu.VMEM((rows, width + 2 * HD), F32),
            pltpu.VMEM((rows, HD), F32),
            pltpu.VMEM((GROUP,) + block, BF16),
            pltpu.VMEM((2, GROUP, rows, HD), BF16),
            pltpu.VMEM((2, NX) + block, BF16),
            pltpu.VMEM((2, NX, heads, 8, HD), F32),
            pltpu.VMEM((2, NX) + block, BF16),
            pltpu.VMEM((2, NX, heads, 8, HD), F32),
            pltpu.VMEM(block, BF16),
            pltpu.VMEM((heads, 8, HD), F32),
            pltpu.VMEM(block, BF16),
            pltpu.VMEM((heads, 8, HD), F32),
            pltpu.VMEM((2, rows, width), BF16),
            pltpu.VMEM((NY, rows, width), BF16),
            pltpu.VMEM((NY, rows, width), BF16),
            dma((6,)), dma((NY,)), dma((7,)), dma((8,)), dma((NY,)), dma((NY,)),
            dma((7,)), dma((GROUP,)), dma((7,)), dma((GROUP,)),
            dma((2, NX)), dma((2, NX)), dma((2, NX)), dma((2, NX)),
            dma((2,)), dma((2,)), dma, dma, dma((NY,)), dma((NY,)), dma,
        ],
        compiler_params=pltpu.CompilerParams(
            collective_id=0, has_side_effects=True, vmem_limit_bytes=48 << 20
        ),
        name="span_attention",
    )(
        tokens, norm_gain.reshape(8, 1, width), w_query, w_key, w_value, w_out,
        keys_cache, values_cache, cached_lengths, cosine, sine,
    )
    fresh = fresh.reshape(2, 3 * GROUP * rows, HD)
    start = place * slots - length
    token = start + jnp.arange(slots, dtype=jnp.int32)
    written = jnp.logical_and(token >= 0, token < GROUP * rows)[:, None]
    begin = jnp.clip(start + GROUP * rows, 0, 2 * GROUP * rows)

    def update(at, cache):
        window = lax.dynamic_slice(fresh, (at, begin, 0), (1, slots, HD))[0]
        return jnp.where(written, window, cache)

    return projected, update(0, keys_cache), update(1, values_cache)


def solution(mesh):
    return jax.shard_map(
        shards,
        mesh=mesh,
        in_specs=(
            P("seq", "head"), P(), P(None, "head"), P(None, "head"), P(None, "head"),
            P("head", None), P("seq", "head"), P("seq", "head"), P(), P(),
        ),
        out_specs=(P("seq", "head"), P("seq", "head"), P("seq", "head")),
        check_vma=False,
    )
```

```python
import math

import jax
import jax.numpy as jnp
import numpy as np
from jax import lax
from jax.experimental import pallas as pl
from jax.experimental.pallas import tpu as pltpu
from jax.sharding import PartitionSpec as P

HD = 128
NX = 4
NZ = 8
NY = 4
GROUP = 8
NEG = -(2.0**100)
ROPE_BASE = 500000.0
EPS = 1e-05
LOG2E = 1.4426950408889634
F32 = jnp.float32
BF16 = jnp.bfloat16


def digit(number, place):
    value = number
    result = value % 10
    for at in range(1, 8):
        value = value // 10
        flag = (place + 8 - at) // 8 - (place + 7 - at) // 8
        result = result + flag * (value % 10 - number % 10)
    return result


def order_code(digits):
    return sum(d * 10**i for i, d in enumerate(digits))


ORDER = [(0, 0, 0), (0, 0, 1), (0, 1, 0), (1, 0, 0), (1, 1, 0), (1, 0, 1), (1, 1, 1), (0, 1, 1)]
STEP_FORWARD = (3, 5)
STEP_MERGE = 5
CHUNK = 1024
CHUNKS = 2


def kernel(
    tok, gain, wq, wk, wv, wo, kc, vc, freq, lens, offs,
    out, keys_out, values_out,
    x_all, gain_v, freq_v, wq_v, wk_v, wv_v, wo_all, kraw, kT, va, kfT, vfa, acc, ssq,
    cos, sin, fresh_pad, updated, q_all, kv_all, o_buf, l_buf, o_in, l_in,
    oz_out, lz_out, oz_in, lz_in, att_all, pr_out, pr_in, own_part,
    load_sem, own_wo_sem, ag_send, ag_recv, wo_send, wo_recv, pair_send, pair_recv,
    q_send, q_recv, kv_send, kv_recv, o_send, o_recv, l_send, l_recv,
    z_send, z_recv, lz_send, lz_recv, att_send, att_recv, pr_send, pr_recv, out_sem,
):
    rows, width = tok.shape
    heads = width // HD
    slots = kc.shape[0]
    s = lax.axis_index("seq")
    h = lax.axis_index("head")
    x, z = s // NZ, s % NZ
    zhi = z // 4
    request = s % 4
    y, c = h // 2, h % 2
    p = s // 4
    z_peer = x * NZ + (z + 4) % NZ
    pz = z_peer // 4
    sib = y * 2 + (1 - c)
    odd = (x + c) % 2
    to_pair, to_next = 1 + 2 * odd, 3 - 2 * odd
    px = 2 * ((x + to_pair) % NX) + zhi
    part_rows = rows // CHUNKS

    def x_peer(d):
        return ((x + d) % NX) * NZ + z

    def y_peer(d):
        return ((y + d) % NY) * 2 + c

    def remote(src, dst, send, recv, seq, head):
        return pltpu.make_async_remote_copy(
            src_ref=src, dst_ref=dst, send_sem=send, recv_sem=recv,
            device_id=(seq, head), device_id_type=pl.DeviceIdType.MESH,
        )

    loads = [
        pltpu.make_async_copy(tok, x_all.at[h], load_sem.at[0]),
        pltpu.make_async_copy(wq, wq_v, load_sem.at[1]),
        pltpu.make_async_copy(wk, wk_v, load_sem.at[2]),
        pltpu.make_async_copy(wv, wv_v, load_sem.at[3]),
        pltpu.make_async_copy(kc, kraw.at[0], load_sem.at[4]),
        pltpu.make_async_copy(vc, va.at[0, :, pl.ds(0, HD)], load_sem.at[5]),
        pltpu.make_async_copy(gain, gain_v, load_sem.at[6]),
        pltpu.make_async_copy(freq, freq_v, load_sem.at[7]),
    ]
    for load in loads:
        load.start()

    def wo_columns(yy, cc):
        return wo.at[:, pl.ds(pl.multiple_of((yy * 2 + cc) * width, width), width)]

    def wo_rows(yy, cc):
        return wo_all.at[yy, pl.ds(pl.multiple_of(cc * width, width), width), :]

    own_wo = [
        pltpu.make_async_copy(wo_columns(yy, c), wo_rows(yy, c), own_wo_sem.at[yy])
        for yy in range(NY)
    ]
    for load in own_wo:
        load.start()

    barrier = pltpu.get_barrier_semaphore()
    peers = [(s, sib), (z_peer, h)]
    peers += [(s, y_peer(d)) for d in (1, 2, 3)] + [(x_peer(d), h) for d in (1, 2, 3)]
    for seq, head in peers:
        pl.semaphore_signal(
            barrier, inc=1, device_id=(seq, head), device_id_type=pl.DeviceIdType.MESH
        )
    for kind in range(2):
        fresh_pad[kind, pl.ds(0, slots), :] = jnp.zeros((slots, HD), F32)
        fresh_pad[kind, pl.ds(2 * slots, slots), :] = jnp.zeros((slots, HD), F32)
    for side in range(2):
        va[side, :, pl.ds(HD, HD)] = jnp.ones((slots, HD), BF16)
        vfa[side, :, pl.ds(HD, HD)] = jnp.ones((rows, HD), BF16)
    acc[...] = jnp.zeros_like(acc)
    ssq[...] = jnp.zeros_like(ssq)
    l_buf[...] = jnp.zeros_like(l_buf)
    pl.semaphore_wait(barrier, len(peers))

    def ag_copy(k, source, seq, head, src=None):
        return remote(
            x_all.at[source] if src is None else src, x_all.at[source],
            ag_send.at[k], ag_recv.at[source], seq, head,
        )

    for k, d in enumerate((2, 1, 3)):
        ag_copy(k, h, s, y_peer(d), tok).start()
    ag_copy(3, h, s, sib, tok).start()
    wo_copies = [
        remote(wo_columns(yy, 1 - c), wo_rows(yy, c), wo_send.at[yy], wo_recv.at[yy], s, sib)
        for yy in range(NY)
    ]
    for copy in wo_copies:
        copy.start()

    pair_copies = [
        remote(kc, kraw.at[1], pair_send.at[0], pair_recv.at[0], x_peer(to_pair), h),
        remote(vc, va.at[1, :, pl.ds(0, HD)], pair_send.at[1], pair_recv.at[1], x_peer(to_pair), h),
    ]
    for copy in pair_copies:
        copy.start()

    length = lens[request]

    def prepare_keys(side, holder):
        for at in range(0, slots, 512):
            kT[side, pl.ds(0, HD), pl.ds(at, 512)] = kraw[side, pl.ds(at, 512), :].T
        slot = holder * slots + lax.broadcasted_iota(jnp.int32, (HD, slots), 1)
        first_row = lax.broadcasted_iota(jnp.int32, (HD, slots), 0) == 0
        hidden = jnp.logical_and(first_row, slot >= length)
        kT[side, pl.ds(HD, HD), :] = jnp.where(hidden, NEG, 0.0).astype(BF16)

    loads[4].wait()
    loads[5].wait()
    prepare_keys(0, p)
    for at in (0, 1, 2, 3, 6, 7):
        loads[at].wait()
    place = offs[request] + length + p * rows
    place = place + lax.broadcasted_iota(jnp.int32, (rows, HD), 0)
    angles = place.astype(F32) * freq_v[...]
    sign = jnp.where(lax.broadcasted_iota(jnp.int32, (rows, HD), 1) < HD // 2, -1.0, 1.0)
    cos[...] = jnp.cos(angles)
    sin[...] = jnp.sin(angles) * sign

    def project(step, unused):
        d = digit(order_code([0, 0, 1, 3, 2, 1, 3, 2]), step)
        other = digit(order_code([0, 1, 0, 0, 0, 1, 1, 1]), step)
        source = ((y + d) % NY) * 2 + (c + other) % 2

        @pl.when(step > 0)
        def _():
            ag_copy(0, source, s, sib).wait_recv()

        @pl.when(jnp.logical_and(step >= 2, step < 5))
        def _():
            ag_copy(2 + step, source, s, sib).start()

        shard = x_all[source].astype(F32)
        square = shard * shard
        ssq[...] += square[:, :HD] + square[:, HD:2 * HD] + square[:, 2 * HD:]
        scaled = (shard * gain_v[source]).astype(BF16)
        at = pl.ds(pl.multiple_of(source * width, width), width)
        acc[:, pl.ds(0, width)] += jnp.dot(scaled, wq_v[at, :], preferred_element_type=F32)
        acc[:, pl.ds(width, HD)] += jnp.dot(scaled, wk_v[at, :], preferred_element_type=F32)
        acc[:, pl.ds(width + HD, HD)] += jnp.dot(scaled, wv_v[at, :], preferred_element_type=F32)
        return unused

    lax.fori_loop(0, 8, project, 0)

    scale = lax.rsqrt(jnp.sum(ssq[...], -1, keepdims=True) * (1.0 / (width * 8)) + EPS)
    cosine = cos[...]
    sine = sin[...]

    def rope(vectors):
        return vectors * cosine + pltpu.roll(vectors, HD // 2, 1) * sine

    def kv_copy(k, block, seq):
        return remote(
            kv_all.at[:, block], kv_all.at[:, block], kv_send.at[k], kv_recv.at[block], seq, h
        )

    fresh_key = rope(acc[:, pl.ds(width, HD)] * scale).astype(BF16)
    fresh_value = (acc[:, pl.ds(width + HD, HD)] * scale).astype(BF16)
    kv_all[0, p] = fresh_key
    kv_all[1, p] = fresh_value
    kv_copy(1, p, x_peer(to_pair)).start()

    def q_copy(k, dz, j, r, to_z, seq):
        return remote(
            q_all.at[dz, 0, r], q_all.at[to_z, j, r], q_send.at[k, r], q_recv.at[to_z, j, r], seq, h
        )

    fold = LOG2E / math.sqrt(HD)
    for r in range(CHUNKS):
        window = pl.ds(r * part_rows, part_rows)
        for hd in range(heads):
            vectors = acc[window, pl.ds(hd * HD, HD)] * scale[r * part_rows:(r + 1) * part_rows]
            turned = vectors * cos[window, :] + pltpu.roll(vectors, HD // 2, 1) * sin[window, :]
            q_all[0, 0, r, pl.ds(hd * part_rows, part_rows), :] = (turned * fold).astype(BF16)
        q_copy(0, 0, 0, r, 1, z_peer).start()
        q_copy(1, 0, 1, r, 0, x_peer(to_next)).start()
    kv_copy(0, p, z_peer).start()

    kfT[0] = fresh_key.T
    vfa[0, :, pl.ds(0, HD)] = fresh_value
    for copy in pair_copies:
        copy.wait_recv()
    prepare_keys(1, px)
    kv_copy(1, px, z_peer).wait_recv()
    kfT[1] = kv_all[0, px].T
    vfa[1, :, pl.ds(0, HD)] = kv_all[1, px]

    eye = lax.broadcasted_iota(jnp.int32, (HD, HD), 0) == lax.broadcasted_iota(
        jnp.int32, (HD, HD), 1
    )
    first_lane = lax.broadcasted_iota(jnp.int32, (part_rows, HD), 1) == 0
    one_lane = jnp.where(first_lane, 1.0, 0.0).astype(BF16)
    offset = lax.broadcasted_iota(jnp.int32, (part_rows, rows), 0) - lax.broadcasted_iota(
        jnp.int32, (part_rows, rows), 1
    )

    def o_copies(dz, r):
        return (
            remote(o_buf.at[dz, 1, r], o_in.at[dz, r], o_send.at[dz, r], o_recv.at[dz, r],
                   x_peer(to_next), h),
            remote(l_buf.at[dz, 1, r], l_in.at[dz, r], l_send.at[dz, r], l_recv.at[dz, r],
                   x_peer(to_next), h),
        )

    def z_copies(r):
        return (
            remote(oz_out.at[r], oz_in.at[r], z_send.at[r], z_recv.at[r], z_peer, h),
            remote(lz_out.at[r], lz_in.at[r], lz_send.at[r], lz_recv.at[r], z_peer, h),
        )

    def weigh(logsums):
        highest = logsums[0]
        for one in logsums[1:]:
            highest = jnp.maximum(highest, one)
        shares = [jnp.exp2(one - highest) for one in logsums]
        total = shares[0]
        for one in shares[1:]:
            total = total + one
        return [one / total for one in shares], highest + jnp.log(total) * LOG2E

    def blend(parts, shares, hd):
        result = None
        for part, share in zip(parts, shares):
            column = jnp.sum(jnp.where(eye, share[hd:hd + 1, :], 0.0), 1, keepdims=True)
            term = part[pl.ds(hd * part_rows, part_rows), :].astype(F32) * column
            result = term if result is None else result + term
        return result

    def merge_for_z(r):
        for copy in o_copies(1, r):
            copy.wait_recv()
        shares, merged = weigh([l_buf[1, 0, r], l_in[1, r]])
        lz_out[r] = merged
        for hd in range(heads):
            oz_out[r, pl.ds(hd * part_rows, part_rows), :] = blend(
                [o_buf.at[1, 0, r], o_in.at[1, r]], shares, hd
            ).astype(BF16)
        for copy in z_copies(r):
            copy.start()

    def attend(step, unused):
        dz = digit(order_code([o[0] for o in ORDER]), step)
        j = digit(order_code([o[1] for o in ORDER]), step)
        r = digit(order_code([o[2] for o in ORDER]), step)
        block = 2 * ((x + j * to_next) % NX) + (zhi + dz) % 2

        for chunk in range(CHUNKS):
            @pl.when(step == STEP_FORWARD[chunk])
            def _():
                q_copy(0, 0, 0, chunk, 1, z_peer).wait_recv()
                q_copy(2, 1, 1, chunk, 1, x_peer(to_next)).start()

        @pl.when(j > 0)
        def _():
            q_copy(1, 0, 1, r, dz, z_peer).wait_recv()

        ahead = [
            offset + r * part_rows + (block - holder) * rows >= 0 for holder in (p, px)
        ]

        def score(hd, side):
            query = q_all[dz, j, r, pl.ds(hd * part_rows, part_rows), :]
            wide = jnp.concatenate([query, one_lane], 1)
            scores = [
                jnp.dot(wide, kT[side, :, pl.ds(at, CHUNK)], preferred_element_type=F32)
                for at in range(0, slots, CHUNK)
            ]
            fresh = jnp.dot(query, kfT[side], preferred_element_type=F32)
            scores.append(jnp.where(ahead[side], fresh, NEG))
            top = jnp.max(scores[0], -1, keepdims=True)
            for part in scores[1:]:
                top = jnp.maximum(top, jnp.max(part, -1, keepdims=True))
            return scores, top

        def weigh_values(side, scores, top):
            values = [va[side, pl.ds(at, CHUNK), :] for at in range(0, slots, CHUNK)]
            summed = None
            for part, value in zip(scores, values + [vfa[side]]):
                weights = jnp.exp2(part - top).astype(BF16)
                term = jnp.dot(weights, value, preferred_element_type=F32)
                summed = term if summed is None else summed + term
            return summed, top

        pieces = [(hd, side) for hd in range(heads) for side in range(2)]
        current = score(*pieces[0])
        halves = []
        for at, (hd, side) in enumerate(pieces):
            following = score(*pieces[at + 1]) if at + 1 < len(pieces) else None
            halves.append(weigh_values(side, *current))
            current = following
            if side == 1:
                (first, first_top), (second, second_top) = halves
                halves = []
                top = jnp.maximum(first_top, second_top)
                summed = first * jnp.exp2(first_top - top) + second * jnp.exp2(second_top - top)
                total = summed[:, HD:]
                o_buf[dz, j, r, pl.ds(hd * part_rows, part_rows), :] = (
                    summed[:, :HD] / total
                ).astype(BF16)
                l_buf[dz, j, r, pl.ds(hd, 1), :] = jnp.sum(
                    jnp.where(eye, top + jnp.log(total) * LOG2E, 0.0), 0, keepdims=True
                )

        @pl.when(j > 0)
        def _():
            for copy in o_copies(dz, r):
                copy.start()

        @pl.when(step == STEP_MERGE)
        def _():
            merge_for_z(0)

        return unused

    lax.fori_loop(0, len(ORDER), attend, 0)
    merge_for_z(1)

    others = (to_pair, to_next, 2)
    for k, d in ((2, to_next), (3, 2)):
        kv_copy(k, p, x_peer(d)).start()
    kv_copy(0, pz, z_peer).wait_recv()
    for k, d in enumerate(others):
        kv_copy(4 + k, pz, x_peer(d)).start()

    for load in own_wo:
        load.wait()
    for copy in wo_copies:
        copy.wait_recv()

    def att_copy(r, core):
        return remote(
            att_all.at[r, core], att_all.at[r, core], att_send.at[r], att_recv.at[r], s, sib
        )

    def pr_copy(r, d):
        back = (NY - d) % NY
        return remote(
            pr_out.at[r, d], pr_in.at[r, back], pr_send.at[r, d], pr_recv.at[r, back], s, y_peer(d)
        )

    for r in range(CHUNKS):
        for copy in o_copies(0, r):
            copy.wait_recv()
        for copy in z_copies(r):
            copy.wait_recv()
        shares, merged = weigh([l_buf[0, 0, r], l_in[0, r], lz_in[r]])
        for hd in range(heads):
            att_all[r, c, :, pl.ds(hd * HD, HD)] = blend(
                [o_buf.at[0, 0, r], o_in.at[0, r], oz_in.at[r]], shares, hd
            ).astype(BF16)
        att_copy(r, c).start()
        att_copy(r, 1 - c).wait_recv()
        both = jnp.concatenate([att_all[r, 0], att_all[r, 1]], 1)
        for d in (2, 1, 3):
            part = jnp.dot(both, wo_all[(y + d) % NY], preferred_element_type=F32)
            pr_out[r, d] = part.astype(BF16)
            pr_copy(r, d).start()
        own_part[r] = jnp.dot(both, wo_all[y], preferred_element_type=F32)

    for d in (to_next, 2):
        kv_copy(0, 2 * ((x + d) % NX) + zhi, z_peer).wait_recv()
    for d in others:
        kv_copy(0, 2 * ((x + d) % NX) + (zhi + 1) % 2, z_peer).wait_recv()
    for kind in range(2):
        for block in range(GROUP):
            fresh_pad[kind, pl.ds(slots + block * rows, rows), :] = kv_all[kind, block].astype(F32)
    start = p * slots - length
    begin = jnp.clip(start + slots, 0, 2 * slots)

    def place_rows(i, unused):
        at = pl.ds(pl.multiple_of(i * rows, rows), rows)
        token = start + i * rows + lax.broadcasted_iota(jnp.int32, (rows, HD), 0)
        written = jnp.logical_and(token >= 0, token < GROUP * rows)
        window = pl.ds(begin + i * rows, rows)
        for kind in range(2):
            cached = kraw[0, at, :] if kind == 0 else va[0, at, pl.ds(0, HD)]
            fresh = fresh_pad[kind, window, :].astype(BF16)
            updated[kind, at, :] = jnp.where(written, fresh, cached)
        return unused

    lax.fori_loop(0, GROUP, place_rows, 0)
    stores = [
        pltpu.make_async_copy(updated.at[0], keys_out, out_sem.at[0]),
        pltpu.make_async_copy(updated.at[1], values_out, out_sem.at[1]),
    ]
    for store in stores:
        store.start()

    for r in range(CHUNKS):
        result = own_part[r]
        for d in (1, 3, 2):
            pr_copy(r, (NY - d) % NY).wait_recv()
        for d in (1, 2, 3):
            result = result + pr_in[r, d].astype(F32)
        out[pl.ds(r * part_rows, part_rows), :] = result.astype(BF16)

    for k in range(3):
        ag_copy(k, h, s, sib, tok).wait_send()
    ag_copy(3, h, s, sib, tok).wait_send()
    for k in range(4, 7):
        ag_copy(k, h, s, sib).wait_send()
    for copy in wo_copies:
        copy.wait_send()
    for copy in pair_copies:
        copy.wait_send()
    for k in range(7):
        kv_copy(k, p, z_peer).wait_send()
    for r in range(CHUNKS):
        for k in range(3):
            q_copy(k, 0, 0, r, 1, z_peer).wait_send()
        for copy in o_copies(0, r) + o_copies(1, r) + z_copies(r):
            copy.wait_send()
        att_copy(r, c).wait_send()
        for d in (1, 2, 3):
            pr_copy(r, d).wait_send()
    for store in stores:
        store.wait()


def hand_on(*refs):
    sems = refs[6]
    copies = [pltpu.make_async_copy(refs[0], refs[3], sems.at[8])]
    for at in (1, 2):
        share = refs[at].shape[0] // 4
        for quarter in range(4):
            window = pl.ds(quarter * share, share)
            copies.append(
                pltpu.make_async_copy(
                    refs[at].at[window], refs[at + 3].at[window], sems.at[4 * at - 4 + quarter]
                )
            )
    for copy in copies:
        copy.start()
    for copy in copies:
        copy.wait()


def shards(
    tokens, norm_gain, w_query, w_key, w_value, w_out, keys_cache, values_cache,
    cached_lengths, rope_offsets,
):
    rows, width = tokens.shape
    slots = keys_cache.shape[0]
    heads = width // HD
    half = np.arange(HD) % (HD // 2)
    frequency = (ROPE_BASE ** (-half * 2.0 / HD)).astype(np.float32)[None]

    hbm_spec = pl.BlockSpec(memory_space=pltpu.HBM)
    vmem_spec = pl.BlockSpec(memory_space=pltpu.VMEM)
    smem_spec = pl.BlockSpec(memory_space=pltpu.SMEM)
    dma = pltpu.SemaphoreType.DMA
    block = (heads * rows // CHUNKS, HD)
    results = pl.pallas_call(
        kernel,
        out_shape=(
            jax.ShapeDtypeStruct((rows, width), BF16),
            jax.ShapeDtypeStruct((slots, HD), BF16),
            jax.ShapeDtypeStruct((slots, HD), BF16),
        ),
        in_specs=[hbm_spec] * 9 + [smem_spec] * 2,
        out_specs=(vmem_spec, hbm_spec, hbm_spec),
        scratch_shapes=[
            pltpu.VMEM((8, rows, width), BF16),
            pltpu.VMEM((8, 1, width), F32),
            pltpu.VMEM((1, HD), F32),
            pltpu.VMEM(w_query.shape, BF16),
            pltpu.VMEM(w_key.shape, BF16),
            pltpu.VMEM(w_value.shape, BF16),
            pltpu.VMEM((NY, 2 * width, width), BF16),
            pltpu.VMEM((2, slots, HD), BF16),
            pltpu.VMEM((2, 2 * HD, slots), BF16),
            pltpu.VMEM((2, slots, 2 * HD), BF16),
            pltpu.VMEM((2, HD, rows), BF16),
            pltpu.VMEM((2, rows, 2 * HD), BF16),
            pltpu.VMEM((rows, width + 2 * HD), F32),
            pltpu.VMEM((rows, HD), F32),
            pltpu.VMEM((rows, HD), F32),
            pltpu.VMEM((rows, HD), F32),
            pltpu.VMEM((2, 3 * slots, HD), F32),
            pltpu.VMEM((2, slots, HD), BF16),
            pltpu.VMEM((2, 2, CHUNKS) + block, BF16),
            pltpu.VMEM((2, GROUP, rows, HD), BF16),
            pltpu.VMEM((2, 2, CHUNKS) + block, BF16),
            pltpu.VMEM((2, 2, CHUNKS, 8, HD), F32),
            pltpu.VMEM((2, CHUNKS) + block, BF16),
            pltpu.VMEM((2, CHUNKS, 8, HD), F32),
            pltpu.VMEM((CHUNKS,) + block, BF16),
            pltpu.VMEM((CHUNKS, 8, HD), F32),
            pltpu.VMEM((CHUNKS,) + block, BF16),
            pltpu.VMEM((CHUNKS, 8, HD), F32),
            pltpu.VMEM((CHUNKS, 2, rows // CHUNKS, width), BF16),
            pltpu.VMEM((CHUNKS, NY, rows // CHUNKS, width), BF16),
            pltpu.VMEM((CHUNKS, NY, rows // CHUNKS, width), BF16),
            pltpu.VMEM((CHUNKS, rows // CHUNKS, width), F32),
            dma((8,)), dma((NY,)), dma((7,)), dma((8,)), dma((NY,)), dma((NY,)), dma((2,)), dma((2,)),
            dma((3, CHUNKS)), dma((2, 2, CHUNKS)), dma((7,)), dma((GROUP,)),
            dma((2, CHUNKS)), dma((2, CHUNKS)), dma((2, CHUNKS)), dma((2, CHUNKS)),
            dma((CHUNKS,)), dma((CHUNKS,)), dma((CHUNKS,)), dma((CHUNKS,)),
            dma((CHUNKS,)), dma((CHUNKS,)), dma((CHUNKS, NY)), dma((CHUNKS, NY)), dma((2,)),
        ],
        compiler_params=pltpu.CompilerParams(
            collective_id=0, has_side_effects=True, vmem_limit_bytes=64 << 20
        ),
        name="span_attention",
    )(
        tokens, norm_gain.reshape(8, 1, width), w_query, w_key, w_value, w_out,
        keys_cache, values_cache, frequency, cached_lengths, rope_offsets,
    )
    return pl.pallas_call(
        hand_on,
        out_shape=tuple(jax.ShapeDtypeStruct(one.shape, one.dtype) for one in results),
        in_specs=[hbm_spec] * 3,
        out_specs=(hbm_spec,) * 3,
        scratch_shapes=[dma((9,))],
        name="hand_on",
    )(*results)


def solution(mesh):
    return jax.shard_map(
        shards,
        mesh=mesh,
        in_specs=(
            P("seq", "head"), P(), P(None, "head"), P(None, "head"), P(None, "head"),
            P("head", None), P("seq", "head"), P("seq", "head"), P(), P(),
        ),
        out_specs=(P("seq", "head"), P("seq", "head"), P("seq", "head")),
        check_vma=False,
    )
```

```python
import math

import jax
import jax.numpy as jnp
import numpy as np
from jax import lax
from jax.experimental import pallas as pl
from jax.experimental.pallas import tpu as pltpu
from jax.sharding import PartitionSpec as P

HD = 128
NX = 4
NZ = 8
NY = 4
GROUP = 8
NEG = -(2.0**100)
ROPE_BASE = 500000.0
EPS = 1e-05
LOG2E = 1.4426950408889634
F32 = jnp.float32
BF16 = jnp.bfloat16


def digit(number, place):
    value = number
    result = value % 10
    for at in range(1, 16):
        value = value // 10
        flag = (place + 16 - at) // 16 - (place + 15 - at) // 16
        result = result + flag * (value % 10 - number % 10)
    return result


def order_code(digits):
    return sum(d * 10**i for i, d in enumerate(digits))


ORDER = [(0, 0, 0), (0, 0, 1), (0, 0, 2), (0, 0, 3)]
ORDER += [(1, j, r) for r in range(4) for j in range(2)]
ORDER += [(0, 1, 0), (0, 1, 1), (0, 1, 2), (0, 1, 3)]
STEP_FORWARD = (3, 4, 6, 8)
STEP_MERGE = (7, 9, 11, 13)
CHUNK = 1024
CHUNKS = 4
GROUPS = 2


def kernel(
    tok, gain, wq, wk, wv, wo, kc, vc, freq, lens, offs,
    out, keys_out, values_out,
    x_all, gain_v, freq_v, wq_v, wk_v, wv_v, wo_all, kraw, kT, va, kfT, vfa, acc, ssq,
    cos, sin, fresh_pad, updated, q_all, kv_all, o_buf, l_buf, o_in, l_in,
    oz_out, lz_out, oz_in, lz_in, att_all, pr_out, pr_in, own_part,
    load_sem, own_wo_sem, ag_send, ag_recv, wo_send, wo_recv, pair_send, pair_recv,
    q_send, q_recv, kv_send, kv_recv, o_send, o_recv, l_send, l_recv,
    z_send, z_recv, lz_send, lz_recv, att_send, att_recv, pr_send, pr_recv, out_sem,
):
    rows, width = tok.shape
    heads = width // HD
    slots = kc.shape[0]
    s = lax.axis_index("seq")
    h = lax.axis_index("head")
    x, z = s // NZ, s % NZ
    zhi = z // 4
    request = s % 4
    y, c = h // 2, h % 2
    p = s // 4
    z_peer = x * NZ + (z + 4) % NZ
    pz = z_peer // 4
    sib = y * 2 + (1 - c)
    odd = (x + c) % 2
    to_pair, to_next = 1 + 2 * odd, 3 - 2 * odd
    px = 2 * ((x + to_pair) % NX) + zhi
    part_rows = rows // CHUNKS

    def x_peer(d):
        return ((x + d) % NX) * NZ + z

    def y_peer(d):
        return ((y + d) % NY) * 2 + c

    def remote(src, dst, send, recv, seq, head):
        return pltpu.make_async_remote_copy(
            src_ref=src, dst_ref=dst, send_sem=send, recv_sem=recv,
            device_id=(seq, head), device_id_type=pl.DeviceIdType.MESH,
        )

    loads = [
        pltpu.make_async_copy(tok, x_all.at[h], load_sem.at[0]),
        pltpu.make_async_copy(wq, wq_v, load_sem.at[1]),
        pltpu.make_async_copy(wk, wk_v, load_sem.at[2]),
        pltpu.make_async_copy(wv, wv_v, load_sem.at[3]),
        pltpu.make_async_copy(kc, kraw.at[0], load_sem.at[4]),
        pltpu.make_async_copy(vc, va.at[0, :, pl.ds(0, HD)], load_sem.at[5]),
        pltpu.make_async_copy(gain, gain_v, load_sem.at[6]),
        pltpu.make_async_copy(freq, freq_v, load_sem.at[7]),
    ]
    loads[0].start()

    def wo_columns(yy, cc):
        return wo.at[:, pl.ds(pl.multiple_of((yy * 2 + cc) * width, width), width)]

    def wo_rows(yy, cc):
        return wo_all.at[yy, pl.ds(pl.multiple_of(cc * width, width), width), :]

    own_wo = [
        pltpu.make_async_copy(wo_columns(yy, c), wo_rows(yy, c), own_wo_sem.at[yy])
        for yy in range(NY)
    ]
    barrier = pltpu.get_barrier_semaphore()
    peers = [(s, sib), (z_peer, h)]
    peers += [(s, y_peer(d)) for d in (1, 2, 3)] + [(x_peer(d), h) for d in (1, 2, 3)]
    for seq, head in peers:
        pl.semaphore_signal(
            barrier, inc=1, device_id=(seq, head), device_id_type=pl.DeviceIdType.MESH
        )
    for kind in range(2):
        fresh_pad[kind, pl.ds(0, slots), :] = jnp.zeros((slots, HD), F32)
        fresh_pad[kind, pl.ds(2 * slots, slots), :] = jnp.zeros((slots, HD), F32)
    for side in range(2):
        va[side, :, pl.ds(HD, HD)] = jnp.ones((slots, HD), BF16)
        vfa[side, :, pl.ds(HD, HD)] = jnp.ones((rows, HD), BF16)
    acc[...] = jnp.zeros_like(acc)
    ssq[...] = jnp.zeros_like(ssq)
    l_buf[...] = jnp.zeros_like(l_buf)
    pl.semaphore_wait(barrier, len(peers))

    def ag_copy(k, source, seq, head, src=None):
        return remote(
            x_all.at[source] if src is None else src, x_all.at[source],
            ag_send.at[k], ag_recv.at[source], seq, head,
        )

    for k, d in enumerate((2, 1, 3)):
        ag_copy(k, h, s, y_peer(d), tok).start()
    ag_copy(3, h, s, sib, tok).start()
    wo_copies = [
        remote(wo_columns(yy, 1 - c), wo_rows(yy, c), wo_send.at[yy], wo_recv.at[yy], s, sib)
        for yy in range(NY)
    ]
    pair_copies = [
        remote(kc, kraw.at[1], pair_send.at[0], pair_recv.at[0], x_peer(to_pair), h),
        remote(vc, va.at[1, :, pl.ds(0, HD)], pair_send.at[1], pair_recv.at[1], x_peer(to_pair), h),
    ]
    for copy in pair_copies:
        copy.start()
    for load in loads[1:] + own_wo:
        load.start()

    length = lens[request]

    def prepare_keys(side, holder):
        for at in range(0, slots, 512):
            kT[side, pl.ds(0, HD), pl.ds(at, 512)] = kraw[side, pl.ds(at, 512), :].T
        slot = holder * slots + lax.broadcasted_iota(jnp.int32, (HD, slots), 1)
        first_row = lax.broadcasted_iota(jnp.int32, (HD, slots), 0) == 0
        hidden = jnp.logical_and(first_row, slot >= length)
        kT[side, pl.ds(HD, HD), :] = jnp.where(hidden, NEG, 0.0).astype(BF16)

    loads[4].wait()
    loads[5].wait()
    prepare_keys(0, p)
    for at in (0, 1, 2, 3, 6, 7):
        loads[at].wait()
    place = offs[request] + length + p * rows
    place = place + lax.broadcasted_iota(jnp.int32, (rows, HD), 0)
    angles = place.astype(F32) * freq_v[...]
    sign = jnp.where(lax.broadcasted_iota(jnp.int32, (rows, HD), 1) < HD // 2, -1.0, 1.0)
    cos[...] = jnp.cos(angles)
    sin[...] = jnp.sin(angles) * sign

    def project(step, unused):
        d = digit(order_code([0, 0, 1, 3, 2, 1, 3, 2]), step)
        other = digit(order_code([0, 1, 0, 0, 0, 1, 1, 1]), step)
        source = ((y + d) % NY) * 2 + (c + other) % 2

        @pl.when(step > 0)
        def _():
            ag_copy(0, source, s, sib).wait_recv()

        @pl.when(jnp.logical_and(step >= 2, step < 5))
        def _():
            ag_copy(2 + step, source, s, sib).start()

        shard = x_all[source].astype(F32)
        square = shard * shard
        ssq[...] += square[:, :HD] + square[:, HD:2 * HD] + square[:, 2 * HD:]
        scaled = (shard * gain_v[source]).astype(BF16)
        at = pl.ds(pl.multiple_of(source * width, width), width)
        acc[:, pl.ds(0, width)] += jnp.dot(scaled, wq_v[at, :], preferred_element_type=F32)
        acc[:, pl.ds(width, HD)] += jnp.dot(scaled, wk_v[at, :], preferred_element_type=F32)
        acc[:, pl.ds(width + HD, HD)] += jnp.dot(scaled, wv_v[at, :], preferred_element_type=F32)
        return unused

    lax.fori_loop(0, 8, project, 0)

    scale = lax.rsqrt(jnp.sum(ssq[...], -1, keepdims=True) * (1.0 / (width * 8)) + EPS)
    cosine = cos[...]
    sine = sin[...]

    def rope(vectors):
        return vectors * cosine + pltpu.roll(vectors, HD // 2, 1) * sine

    def kv_copy(k, block, seq):
        return remote(
            kv_all.at[:, block], kv_all.at[:, block], kv_send.at[k], kv_recv.at[block], seq, h
        )

    fresh_key = rope(acc[:, pl.ds(width, HD)] * scale).astype(BF16)
    fresh_value = (acc[:, pl.ds(width + HD, HD)] * scale).astype(BF16)
    kv_all[0, p] = fresh_key
    kv_all[1, p] = fresh_value
    kv_copy(1, p, x_peer(to_pair)).start()

    def q_copy(k, dz, j, r, to_z, seq):
        return remote(
            q_all.at[dz, 0, r], q_all.at[to_z, j, r], q_send.at[k, r], q_recv.at[to_z, j, r], seq, h
        )

    fold = LOG2E / math.sqrt(HD)
    for r in range(CHUNKS):
        window = pl.ds(r * part_rows, part_rows)
        for hd in range(heads):
            vectors = acc[window, pl.ds(hd * HD, HD)] * scale[r * part_rows:(r + 1) * part_rows]
            turned = vectors * cos[window, :] + pltpu.roll(vectors, HD // 2, 1) * sin[window, :]
            q_all[0, 0, r, pl.ds(hd * part_rows, part_rows), :] = (turned * fold).astype(BF16)
        q_copy(0, 0, 0, r, 1, z_peer).start()
        q_copy(1, 0, 1, r, 0, x_peer(to_next)).start()
    kv_copy(0, p, z_peer).start()
    for copy in wo_copies:
        copy.start()

    kfT[0] = fresh_key.T
    vfa[0, :, pl.ds(0, HD)] = fresh_value
    for copy in pair_copies:
        copy.wait_recv()
    prepare_keys(1, px)
    kv_copy(1, px, z_peer).wait_recv()
    kfT[1] = kv_all[0, px].T
    vfa[1, :, pl.ds(0, HD)] = kv_all[1, px]

    eye = lax.broadcasted_iota(jnp.int32, (part_rows, HD), 0) == lax.broadcasted_iota(
        jnp.int32, (part_rows, HD), 1
    )
    stacked = heads * part_rows
    first_lane = lax.broadcasted_iota(jnp.int32, (stacked, HD), 1) == 0
    one_lane = jnp.where(first_lane, 1.0, 0.0).astype(BF16)
    offset = lax.broadcasted_iota(jnp.int32, (stacked, rows), 0) % part_rows
    offset = offset - lax.broadcasted_iota(jnp.int32, (stacked, rows), 1)

    def o_copies(dz, r):
        return (
            remote(o_buf.at[dz, 1, r], o_in.at[dz, r], o_send.at[dz, r], o_recv.at[dz, r],
                   x_peer(to_next), h),
            remote(l_buf.at[dz, 1, r], l_in.at[dz, r], l_send.at[dz, r], l_recv.at[dz, r],
                   x_peer(to_next), h),
        )

    def z_copies(r):
        return (
            remote(oz_out.at[r], oz_in.at[r], z_send.at[r], z_recv.at[r], z_peer, h),
            remote(lz_out.at[r], lz_in.at[r], lz_send.at[r], lz_recv.at[r], z_peer, h),
        )

    def weigh(logsums):
        highest = logsums[0]
        for one in logsums[1:]:
            highest = jnp.maximum(highest, one)
        shares = [jnp.exp2(one - highest) for one in logsums]
        total = shares[0]
        for one in shares[1:]:
            total = total + one
        return [one / total for one in shares], highest + jnp.log(total) * LOG2E

    def blend(parts, shares, hd):
        result = None
        for part, share in zip(parts, shares):
            column = jnp.sum(jnp.where(eye, share[hd:hd + 1, :], 0.0), 1, keepdims=True)
            term = part[pl.ds(hd * part_rows, part_rows), :].astype(F32) * column
            result = term if result is None else result + term
        return result

    def merge_for_z(r):
        for copy in o_copies(1, r):
            copy.wait_recv()
        shares, merged = weigh([l_buf[1, 0, r], l_in[1, r]])
        lz_out[r] = merged
        for hd in range(heads):
            oz_out[r, pl.ds(hd * part_rows, part_rows), :] = blend(
                [o_buf.at[1, 0, r], o_in.at[1, r]], shares, hd
            ).astype(BF16)
        for copy in z_copies(r):
            copy.start()

    def attend(step, unused):
        dz = digit(order_code([o[0] for o in ORDER]), step)
        j = digit(order_code([o[1] for o in ORDER]), step)
        r = digit(order_code([o[2] for o in ORDER]), step)
        block = 2 * ((x + j * to_next) % NX) + (zhi + dz) % 2

        for chunk in range(CHUNKS):
            @pl.when(step == STEP_FORWARD[chunk])
            def _():
                q_copy(0, 0, 0, chunk, 1, z_peer).wait_recv()
                q_copy(2, 1, 1, chunk, 1, x_peer(to_next)).start()

        @pl.when(j > 0)
        def _():
            q_copy(1, 0, 1, r, dz, z_peer).wait_recv()

        ahead = [
            offset + r * part_rows + (block - holder) * rows >= 0 for holder in (p, px)
        ]

        query = q_all[dz, j, r]
        wide = jnp.concatenate([query, one_lane], 1)

        def score(side, at):
            scores = [jnp.dot(wide, kT[side, :, pl.ds(at, CHUNK)], preferred_element_type=F32)]
            if at + CHUNK == slots:
                fresh = jnp.dot(query, kfT[side], preferred_element_type=F32)
                scores.append(jnp.where(ahead[side], fresh, NEG))
            top = jnp.max(scores[0], -1, keepdims=True)
            for part in scores[1:]:
                top = jnp.maximum(top, jnp.max(part, -1, keepdims=True))
            return scores, top

        def weigh_values(side, at, scores, top):
            summed = None
            for part, value in zip(scores, (va[side, pl.ds(at, CHUNK), :], vfa[side])):
                weights = jnp.exp2(part - top).astype(BF16)
                term = jnp.dot(weights, value, preferred_element_type=F32)
                summed = term if summed is None else summed + term
            return summed, top

        pieces = [(side, at) for side in range(2) for at in range(0, slots, CHUNK)]
        current = score(*pieces[0])
        sums = []
        for number, piece in enumerate(pieces):
            following = score(*pieces[number + 1]) if number + 1 < len(pieces) else None
            sums.append(weigh_values(*piece, *current))
            current = following
        top = sums[0][1]
        for one, one_top in sums[1:]:
            top = jnp.maximum(top, one_top)
        summed = sums[0][0] * jnp.exp2(sums[0][1] - top)
        for one, one_top in sums[1:]:
            summed = summed + one * jnp.exp2(one_top - top)
        total = summed[:, HD:]
        o_buf[dz, j, r] = (summed[:, :HD] / total).astype(BF16)
        logsum = top + jnp.log(total) * LOG2E
        for hd in range(heads):
            l_buf[dz, j, r, pl.ds(hd, 1), :] = jnp.sum(
                jnp.where(eye, logsum[hd * part_rows:(hd + 1) * part_rows], 0.0), 0, keepdims=True
            )

        @pl.when(j > 0)
        def _():
            for copy in o_copies(dz, r):
                copy.start()

        for chunk in range(CHUNKS):
            @pl.when(step == STEP_MERGE[chunk])
            def _():
                merge_for_z(chunk)

        return unused

    lax.fori_loop(0, len(ORDER), attend, 0)

    others = (to_pair, to_next, 2)
    for k, d in ((2, to_next), (3, 2)):
        kv_copy(k, p, x_peer(d)).start()
    kv_copy(0, pz, z_peer).wait_recv()
    for k, d in enumerate(others):
        kv_copy(4 + k, pz, x_peer(d)).start()

    for load in own_wo:
        load.wait()
    for copy in wo_copies:
        copy.wait_recv()

    def att_copy(r, core):
        return remote(
            att_all.at[r, core], att_all.at[r, core], att_send.at[r], att_recv.at[r], s, sib
        )

    def pr_copy(r, d):
        back = (NY - d) % NY
        return remote(
            pr_out.at[r, d], pr_in.at[r, back], pr_send.at[r, d], pr_recv.at[r, back], s, y_peer(d)
        )

    per_group = CHUNKS // GROUPS
    for g in range(GROUPS):
        for k in range(per_group):
            r = g * per_group + k
            for copy in o_copies(0, r):
                copy.wait_recv()
            for copy in z_copies(r):
                copy.wait_recv()
            shares, merged = weigh([l_buf[0, 0, r], l_in[0, r], lz_in[r]])
            for hd in range(heads):
                att_all[g, c, pl.ds(k * part_rows, part_rows), pl.ds(hd * HD, HD)] = blend(
                    [o_buf.at[0, 0, r], o_in.at[0, r], oz_in.at[r]], shares, hd
                ).astype(BF16)
        att_copy(g, c).start()
        att_copy(g, 1 - c).wait_recv()
        both = jnp.concatenate([att_all[g, 0], att_all[g, 1]], 1)
        for d in (2, 1, 3):
            part = jnp.dot(both, wo_all[(y + d) % NY], preferred_element_type=F32)
            pr_out[g, d] = part.astype(BF16)
            pr_copy(g, d).start()
        own_part[g] = jnp.dot(both, wo_all[y], preferred_element_type=F32)

    for d in (to_next, 2):
        kv_copy(0, 2 * ((x + d) % NX) + zhi, z_peer).wait_recv()
    for d in others:
        kv_copy(0, 2 * ((x + d) % NX) + (zhi + 1) % 2, z_peer).wait_recv()
    for kind in range(2):
        for block in range(GROUP):
            fresh_pad[kind, pl.ds(slots + block * rows, rows), :] = kv_all[kind, block].astype(F32)
    start = p * slots - length
    begin = jnp.clip(start + slots, 0, 2 * slots)

    def place_rows(i, unused):
        at = pl.ds(pl.multiple_of(i * rows, rows), rows)
        token = start + i * rows + lax.broadcasted_iota(jnp.int32, (rows, HD), 0)
        written = jnp.logical_and(token >= 0, token < GROUP * rows)
        window = pl.ds(begin + i * rows, rows)
        for kind in range(2):
            cached = kraw[0, at, :] if kind == 0 else va[0, at, pl.ds(0, HD)]
            fresh = fresh_pad[kind, window, :].astype(BF16)
            updated[kind, at, :] = jnp.where(written, fresh, cached)
        return unused

    lax.fori_loop(0, GROUP, place_rows, 0)
    stores = [
        pltpu.make_async_copy(updated.at[0], keys_out, out_sem.at[0]),
        pltpu.make_async_copy(updated.at[1], values_out, out_sem.at[1]),
    ]
    for store in stores:
        store.start()

    for g in range(GROUPS):
        result = own_part[g]
        for d in (1, 3, 2):
            pr_copy(g, (NY - d) % NY).wait_recv()
        for d in (1, 2, 3):
            result = result + pr_in[g, d].astype(F32)
        out[pl.ds(g * (rows // GROUPS), rows // GROUPS), :] = result.astype(BF16)

    for k in range(3):
        ag_copy(k, h, s, sib, tok).wait_send()
    ag_copy(3, h, s, sib, tok).wait_send()
    for k in range(4, 7):
        ag_copy(k, h, s, sib).wait_send()
    for copy in wo_copies:
        copy.wait_send()
    for copy in pair_copies:
        copy.wait_send()
    for k in range(7):
        kv_copy(k, p, z_peer).wait_send()
    for r in range(CHUNKS):
        for k in range(3):
            q_copy(k, 0, 0, r, 1, z_peer).wait_send()
        for copy in o_copies(0, r) + o_copies(1, r) + z_copies(r):
            copy.wait_send()
    for g in range(GROUPS):
        att_copy(g, c).wait_send()
        for d in (1, 2, 3):
            pr_copy(g, d).wait_send()
    for store in stores:
        store.wait()


def hand_on(*refs):
    sources, targets, held, (in_sem, out_sem) = refs[:3], refs[3:6], refs[6:9], refs[9:]
    pieces = []
    for at, source in enumerate(sources):
        share = source.shape[0] // 2
        pieces += [(at, half, pl.ds(half * share, share)) for half in range(2)]
    arriving = [
        pltpu.make_async_copy(sources[at].at[window], held[at].at[window], in_sem.at[at, half])
        for at, half, window in pieces
    ]
    leaving = [
        pltpu.make_async_copy(held[at].at[window], targets[at].at[window], out_sem.at[at, half])
        for at, half, window in pieces
    ]
    for copy in arriving:
        copy.start()
    for first, second in zip(arriving, leaving):
        first.wait()
        second.start()
    for copy in leaving:
        copy.wait()


def shards(
    tokens, norm_gain, w_query, w_key, w_value, w_out, keys_cache, values_cache,
    cached_lengths, rope_offsets,
):
    rows, width = tokens.shape
    slots = keys_cache.shape[0]
    heads = width // HD
    half = np.arange(HD) % (HD // 2)
    frequency = (ROPE_BASE ** (-half * 2.0 / HD)).astype(np.float32)[None]

    hbm_spec = pl.BlockSpec(memory_space=pltpu.HBM)
    vmem_spec = pl.BlockSpec(memory_space=pltpu.VMEM)
    smem_spec = pl.BlockSpec(memory_space=pltpu.SMEM)
    dma = pltpu.SemaphoreType.DMA
    block = (heads * rows // CHUNKS, HD)
    results = pl.pallas_call(
        kernel,
        out_shape=(
            jax.ShapeDtypeStruct((rows, width), BF16),
            jax.ShapeDtypeStruct((slots, HD), BF16),
            jax.ShapeDtypeStruct((slots, HD), BF16),
        ),
        in_specs=[hbm_spec] * 9 + [smem_spec] * 2,
        out_specs=(vmem_spec, hbm_spec, hbm_spec),
        scratch_shapes=[
            pltpu.VMEM((8, rows, width), BF16),
            pltpu.VMEM((8, 1, width), F32),
            pltpu.VMEM((1, HD), F32),
            pltpu.VMEM(w_query.shape, BF16),
            pltpu.VMEM(w_key.shape, BF16),
            pltpu.VMEM(w_value.shape, BF16),
            pltpu.VMEM((NY, 2 * width, width), BF16),
            pltpu.VMEM((2, slots, HD), BF16),
            pltpu.VMEM((2, 2 * HD, slots), BF16),
            pltpu.VMEM((2, slots, 2 * HD), BF16),
            pltpu.VMEM((2, HD, rows), BF16),
            pltpu.VMEM((2, rows, 2 * HD), BF16),
            pltpu.VMEM((rows, width + 2 * HD), F32),
            pltpu.VMEM((rows, HD), F32),
            pltpu.VMEM((rows, HD), F32),
            pltpu.VMEM((rows, HD), F32),
            pltpu.VMEM((2, 3 * slots, HD), F32),
            pltpu.VMEM((2, slots, HD), BF16),
            pltpu.VMEM((2, 2, CHUNKS) + block, BF16),
            pltpu.VMEM((2, GROUP, rows, HD), BF16),
            pltpu.VMEM((2, 2, CHUNKS) + block, BF16),
            pltpu.VMEM((2, 2, CHUNKS, 8, HD), F32),
            pltpu.VMEM((2, CHUNKS) + block, BF16),
            pltpu.VMEM((2, CHUNKS, 8, HD), F32),
            pltpu.VMEM((CHUNKS,) + block, BF16),
            pltpu.VMEM((CHUNKS, 8, HD), F32),
            pltpu.VMEM((CHUNKS,) + block, BF16),
            pltpu.VMEM((CHUNKS, 8, HD), F32),
            pltpu.VMEM((GROUPS, 2, rows // GROUPS, width), BF16),
            pltpu.VMEM((GROUPS, NY, rows // GROUPS, width), BF16),
            pltpu.VMEM((GROUPS, NY, rows // GROUPS, width), BF16),
            pltpu.VMEM((GROUPS, rows // GROUPS, width), F32),
            dma((8,)), dma((NY,)), dma((7,)), dma((8,)), dma((NY,)), dma((NY,)), dma((2,)), dma((2,)),
            dma((3, CHUNKS)), dma((2, 2, CHUNKS)), dma((7,)), dma((GROUP,)),
            dma((2, CHUNKS)), dma((2, CHUNKS)), dma((2, CHUNKS)), dma((2, CHUNKS)),
            dma((CHUNKS,)), dma((CHUNKS,)), dma((CHUNKS,)), dma((CHUNKS,)),
            dma((GROUPS,)), dma((GROUPS,)), dma((GROUPS, NY)), dma((GROUPS, NY)), dma((2,)),
        ],
        compiler_params=pltpu.CompilerParams(
            collective_id=0, has_side_effects=True, vmem_limit_bytes=64 << 20
        ),
        name="span_attention",
    )(
        tokens, norm_gain.reshape(8, 1, width), w_query, w_key, w_value, w_out,
        keys_cache, values_cache, frequency, cached_lengths, rope_offsets,
    )
    return pl.pallas_call(
        hand_on,
        out_shape=tuple(jax.ShapeDtypeStruct(one.shape, one.dtype) for one in results),
        in_specs=[hbm_spec] * 3,
        out_specs=(hbm_spec,) * 3,
        scratch_shapes=[pltpu.VMEM(one.shape, one.dtype) for one in results]
        + [dma((3, 2)), dma((3, 2))],
        name="hand_on",
    )(*results)


def solution(mesh):
    return jax.shard_map(
        shards,
        mesh=mesh,
        in_specs=(
            P("seq", "head"), P(), P(None, "head"), P(None, "head"), P(None, "head"),
            P("head", None), P("seq", "head"), P("seq", "head"), P(), P(),
        ),
        out_specs=(P("seq", "head"), P("seq", "head"), P("seq", "head")),
        check_vma=False,
    )
```

```python
import math

import jax
import jax.numpy as jnp
import numpy as np
from jax import lax
from jax.experimental import pallas as pl
from jax.experimental.pallas import tpu as pltpu
from jax.sharding import PartitionSpec as P

HD = 128
NX = 4
NZ = 8
NY = 4
GROUP = 8
NEG = -(2.0**100)
ROPE_BASE = 500000.0
EPS = 1e-05
LOG2E = 1.4426950408889634
F32 = jnp.float32
BF16 = jnp.bfloat16


def digit(number, place):
    value = number
    result = value % 10
    for at in range(1, 16):
        value = value // 10
        flag = (place + 16 - at) // 16 - (place + 15 - at) // 16
        result = result + flag * (value % 10 - number % 10)
    return result


def order_code(digits):
    return sum(d * 10**i for i, d in enumerate(digits))


ORDER = [(0, 0, 0), (0, 0, 1), (0, 1, 0), (0, 1, 1), (1, 0, 0), (1, 1, 0), (1, 1, 1), (1, 0, 1)]
ORDER += [(1, 1, 2), (1, 0, 2), (1, 1, 3), (1, 0, 3), (0, 1, 2), (0, 1, 3), (0, 0, 2), (0, 0, 3)]
LATE_FRESH = 2
STEP_FORWARD = (4, 5, 6, 8)
STEP_MERGE = (6, 8, 10, 11)
STEP_KEYS = 6
STEP_BLEND, STEP_PROJECT = 13, 14
CHUNK = 2048
CHUNKS = 4
GROUPS = 2


def kernel(
    tok, gain, wq, wk, wv, wo, kc, vc, freq, lens, offs,
    out, keys_out, values_out,
    x_all, gain_v, freq_v, wq_v, wk_v, wv_v, wo_all, kraw, kT, va, kfT, vfa, acc, ssq,
    cos, sin, fresh_pad, updated, q_all, kv_all, o_buf, l_buf, o_in, l_in,
    oz_out, lz_out, oz_in, lz_in, att_all, pr_out, pr_in, own_part, late_o, late_l,
    load_sem, own_wo_sem, ag_send, ag_recv, wo_send, wo_recv, pair_send, pair_recv,
    q_send, q_recv, kv_send, kv_recv, o_send, o_recv, l_send, l_recv,
    z_send, z_recv, lz_send, lz_recv, att_send, att_recv, pr_send, pr_recv, out_sem,
):
    rows, width = tok.shape
    heads = width // HD
    slots = kc.shape[0]
    s = lax.axis_index("seq")
    h = lax.axis_index("head")
    x, z = s // NZ, s % NZ
    zhi = z // 4
    request = s % 4
    y, c = h // 2, h % 2
    p = s // 4
    z_peer = x * NZ + (z + 4) % NZ
    pz = z_peer // 4
    sib = y * 2 + (1 - c)
    odd = (x + c) % 2
    to_pair, to_next = 1 + 2 * odd, 3 - 2 * odd
    px = 2 * ((x + to_pair) % NX) + zhi
    part_rows = rows // CHUNKS

    def x_peer(d):
        return ((x + d) % NX) * NZ + z

    def y_peer(d):
        return ((y + d) % NY) * 2 + c

    def remote(src, dst, send, recv, seq, head):
        return pltpu.make_async_remote_copy(
            src_ref=src, dst_ref=dst, send_sem=send, recv_sem=recv,
            device_id=(seq, head), device_id_type=pl.DeviceIdType.MESH,
        )

    loads = [
        pltpu.make_async_copy(tok, x_all.at[h], load_sem.at[0]),
        pltpu.make_async_copy(wq, wq_v, load_sem.at[1]),
        pltpu.make_async_copy(wk, wk_v, load_sem.at[2]),
        pltpu.make_async_copy(wv, wv_v, load_sem.at[3]),
        pltpu.make_async_copy(kc, kraw.at[0], load_sem.at[4]),
        pltpu.make_async_copy(vc, va.at[0, :, pl.ds(0, HD)], load_sem.at[5]),
        pltpu.make_async_copy(gain, gain_v, load_sem.at[6]),
        pltpu.make_async_copy(freq, freq_v, load_sem.at[7]),
    ]
    loads[0].start()

    def wo_columns(yy, cc):
        return wo.at[:, pl.ds(pl.multiple_of((yy * 2 + cc) * width, width), width)]

    def wo_rows(yy, cc):
        return wo_all.at[yy, pl.ds(pl.multiple_of(cc * width, width), width), :]

    own_wo = [
        pltpu.make_async_copy(wo_columns(yy, c), wo_rows(yy, c), own_wo_sem.at[yy])
        for yy in range(NY)
    ]
    barrier = pltpu.get_barrier_semaphore()
    peers = [(s, sib), (z_peer, h)]
    peers += [(s, y_peer(d)) for d in (1, 2, 3)] + [(x_peer(d), h) for d in (1, 2, 3)]
    for seq, head in peers:
        pl.semaphore_signal(
            barrier, inc=1, device_id=(seq, head), device_id_type=pl.DeviceIdType.MESH
        )
    for kind in range(2):
        fresh_pad[kind, pl.ds(0, slots), :] = jnp.zeros((slots, HD), F32)
        fresh_pad[kind, pl.ds(2 * slots, slots), :] = jnp.zeros((slots, HD), F32)
    for side in range(2):
        va[side, :, pl.ds(HD, HD)] = jnp.ones((slots, HD), BF16)
        vfa[side, :, pl.ds(HD, HD)] = jnp.ones((rows, HD), BF16)
    acc[...] = jnp.zeros_like(acc)
    ssq[...] = jnp.zeros_like(ssq)
    l_buf[...] = jnp.zeros_like(l_buf)
    late_l[...] = jnp.zeros_like(late_l)
    pl.semaphore_wait(barrier, len(peers))

    def ag_copy(k, source, seq, head, src=None):
        return remote(
            x_all.at[source] if src is None else src, x_all.at[source],
            ag_send.at[k], ag_recv.at[source], seq, head,
        )

    for k, d in enumerate((2, 1, 3)):
        ag_copy(k, h, s, y_peer(d), tok).start()
    ag_copy(3, h, s, sib, tok).start()
    wo_copies = [
        remote(wo_columns(yy, 1 - c), wo_rows(yy, c), wo_send.at[yy], wo_recv.at[yy], s, sib)
        for yy in range(NY)
    ]
    pair_copies = [
        remote(kc, kraw.at[1], pair_send.at[0], pair_recv.at[0], x_peer(to_pair), h),
        remote(vc, va.at[1, :, pl.ds(0, HD)], pair_send.at[1], pair_recv.at[1], x_peer(to_pair), h),
    ]
    for copy in pair_copies:
        copy.start()
    for load in loads[1:] + own_wo:
        load.start()

    length = lens[request]

    def prepare_keys(side, holder):
        for at in range(0, slots, 512):
            kT[side, pl.ds(0, HD), pl.ds(at, 512)] = kraw[side, pl.ds(at, 512), :].T
        slot = holder * slots + lax.broadcasted_iota(jnp.int32, (HD, slots), 1)
        first_row = lax.broadcasted_iota(jnp.int32, (HD, slots), 0) == 0
        hidden = jnp.logical_and(first_row, slot >= length)
        kT[side, pl.ds(HD, HD), :] = jnp.where(hidden, NEG, 0.0).astype(BF16)

    loads[4].wait()
    loads[5].wait()
    prepare_keys(0, p)
    for at in (0, 1, 2, 3, 6, 7):
        loads[at].wait()
    place = offs[request] + length + p * rows
    place = place + lax.broadcasted_iota(jnp.int32, (rows, HD), 0)
    angles = place.astype(F32) * freq_v[...]
    sign = jnp.where(lax.broadcasted_iota(jnp.int32, (rows, HD), 1) < HD // 2, -1.0, 1.0)
    cos[...] = jnp.cos(angles)
    sin[...] = jnp.sin(angles) * sign

    def project(step, unused):
        d = digit(order_code([0, 0, 1, 3, 2, 1, 3, 2]), step)
        other = digit(order_code([0, 1, 0, 0, 0, 1, 1, 1]), step)
        source = ((y + d) % NY) * 2 + (c + other) % 2

        @pl.when(step > 0)
        def _():
            ag_copy(0, source, s, sib).wait_recv()

        @pl.when(jnp.logical_and(step >= 2, step < 5))
        def _():
            ag_copy(2 + step, source, s, sib).start()

        shard = x_all[source].astype(F32)
        square = shard * shard
        ssq[...] += square[:, :HD] + square[:, HD:2 * HD] + square[:, 2 * HD:]
        scaled = (shard * gain_v[source]).astype(BF16)
        at = pl.ds(pl.multiple_of(source * width, width), width)
        acc[:, pl.ds(0, width)] += jnp.dot(scaled, wq_v[at, :], preferred_element_type=F32)
        acc[:, pl.ds(width, HD)] += jnp.dot(scaled, wk_v[at, :], preferred_element_type=F32)
        acc[:, pl.ds(width + HD, HD)] += jnp.dot(scaled, wv_v[at, :], preferred_element_type=F32)
        return unused

    lax.fori_loop(0, 8, project, 0)

    scale = lax.rsqrt(jnp.sum(ssq[...], -1, keepdims=True) * (1.0 / (width * 8)) + EPS)
    cosine = cos[...]
    sine = sin[...]

    def rope(vectors):
        return vectors * cosine + pltpu.roll(vectors, HD // 2, 1) * sine

    def kv_copy(kind, k, block, seq):
        return remote(
            kv_all.at[kind, block], kv_all.at[kind, block],
            kv_send.at[kind, k], kv_recv.at[kind, block], seq, h,
        )

    fresh_key = rope(acc[:, pl.ds(width, HD)] * scale).astype(BF16)
    fresh_value = (acc[:, pl.ds(width + HD, HD)] * scale).astype(BF16)
    kv_all[0, p] = fresh_key
    kv_all[1, p] = fresh_value
    for kind in range(2):
        kv_copy(kind, 1, p, x_peer(to_pair)).start()

    def q_copy(k, dz, j, r, to_z, seq):
        return remote(
            q_all.at[dz, 0, r], q_all.at[to_z, j, r], q_send.at[k, r], q_recv.at[to_z, j, r], seq, h
        )

    fold = LOG2E / math.sqrt(HD)
    for r in range(CHUNKS):
        window = pl.ds(r * part_rows, part_rows)
        for hd in range(heads):
            vectors = acc[window, pl.ds(hd * HD, HD)] * scale[r * part_rows:(r + 1) * part_rows]
            turned = vectors * cos[window, :] + pltpu.roll(vectors, HD // 2, 1) * sin[window, :]
            q_all[0, 0, r, pl.ds(hd * part_rows, part_rows), :] = (turned * fold).astype(BF16)
        q_copy(0, 0, 0, r, 1, z_peer).start()
        q_copy(1, 0, 1, r, 0, x_peer(to_next)).start()
    for copy in wo_copies:
        copy.start()

    kfT[0] = fresh_key.T
    vfa[0, :, pl.ds(0, HD)] = fresh_value
    for copy in pair_copies:
        copy.wait_recv()
    prepare_keys(1, px)
    kfT[1] = jnp.zeros((HD, rows), BF16)
    vfa[1, :, pl.ds(0, HD)] = jnp.zeros((rows, HD), BF16)

    eye = lax.broadcasted_iota(jnp.int32, (part_rows, HD), 0) == lax.broadcasted_iota(
        jnp.int32, (part_rows, HD), 1
    )
    stacked = heads * part_rows
    first_lane = lax.broadcasted_iota(jnp.int32, (stacked, HD), 1) == 0
    one_lane = jnp.where(first_lane, 1.0, 0.0).astype(BF16)
    offset = lax.broadcasted_iota(jnp.int32, (stacked, rows), 0) % part_rows
    offset = offset - lax.broadcasted_iota(jnp.int32, (stacked, rows), 1)

    def o_copies(dz, r):
        return (
            remote(o_buf.at[dz, 1, r], o_in.at[dz, r], o_send.at[dz, r], o_recv.at[dz, r],
                   x_peer(to_next), h),
            remote(l_buf.at[dz, 1, r], l_in.at[dz, r], l_send.at[dz, r], l_recv.at[dz, r],
                   x_peer(to_next), h),
        )

    def z_copies(r):
        return (
            remote(oz_out.at[r], oz_in.at[r], z_send.at[r], z_recv.at[r], z_peer, h),
            remote(lz_out.at[r], lz_in.at[r], lz_send.at[r], lz_recv.at[r], z_peer, h),
        )

    def weigh(logsums):
        highest = logsums[0]
        for one in logsums[1:]:
            highest = jnp.maximum(highest, one)
        shares = [jnp.exp2(one - highest) for one in logsums]
        total = shares[0]
        for one in shares[1:]:
            total = total + one
        return [one / total for one in shares], highest + jnp.log(total) * LOG2E

    def blend(parts, shares, hd):
        result = None
        for part, share in zip(parts, shares):
            column = jnp.sum(jnp.where(eye, share[hd:hd + 1, :], 0.0), 1, keepdims=True)
            term = part[pl.ds(hd * part_rows, part_rows), :].astype(F32) * column
            result = term if result is None else result + term
        return result

    def merge_for_z(r):
        for copy in o_copies(1, r):
            copy.wait_recv()
        shares, merged = weigh([l_buf[1, 0, r], l_in[1, r]])
        lz_out[r] = merged
        for hd in range(heads):
            oz_out[r, pl.ds(hd * part_rows, part_rows), :] = blend(
                [o_buf.at[1, 0, r], o_in.at[1, r]], shares, hd
            ).astype(BF16)
        for copy in z_copies(r):
            copy.start()

    def att_copy(g, core):
        return remote(
            att_all.at[g, core], att_all.at[g, core], att_send.at[g], att_recv.at[g], s, sib
        )

    def pr_copy(g, d):
        back = (NY - d) % NY
        return remote(
            pr_out.at[g, d], pr_in.at[g, back], pr_send.at[g, d], pr_recv.at[g, back], s, y_peer(d)
        )

    def attend_late_fresh():
        for r in range(LATE_FRESH):
            scores = jnp.dot(q_all[0, 0, r], kfT[1], preferred_element_type=F32)
            scores = jnp.where(offset + r * part_rows + (p - px) * rows >= 0, scores, NEG)
            top = jnp.max(scores, -1, keepdims=True)
            weights = jnp.exp2(scores - top).astype(BF16)
            summed = jnp.dot(weights, vfa[1], preferred_element_type=F32)
            total = summed[:, HD:]
            late_o[r] = (summed[:, :HD] / total).astype(BF16)
            logsum = top + jnp.log(total) * LOG2E
            for hd in range(heads):
                late_l[r, pl.ds(hd, 1), :] = jnp.sum(
                    jnp.where(eye, logsum[hd * part_rows:(hd + 1) * part_rows], 0.0),
                    0, keepdims=True,
                )

    per_group = CHUNKS // GROUPS

    def blend_group(g):
        for k in range(per_group):
            r = g * per_group + k
            for copy in o_copies(0, r) + z_copies(r):
                copy.wait_recv()
            parts = [o_buf.at[0, 0, r], o_in.at[0, r], oz_in.at[r]]
            logsums = [l_buf[0, 0, r], l_in[0, r], lz_in[r]]
            if r < LATE_FRESH:
                parts.append(late_o.at[r])
                logsums.append(late_l[r])
            shares, merged = weigh(logsums)
            for hd in range(heads):
                att_all[g, c, pl.ds(k * part_rows, part_rows), pl.ds(hd * HD, HD)] = blend(
                    parts, shares, hd
                ).astype(BF16)
        att_copy(g, c).start()

    def project_group(g):
        if g == 0:
            for load in own_wo:
                load.wait()
            for copy in wo_copies:
                copy.wait_recv()
        att_copy(g, 1 - c).wait_recv()
        both = jnp.concatenate([att_all[g, 0], att_all[g, 1]], 1)
        for d in (2, 1, 3):
            part = jnp.dot(both, wo_all[(y + d) % NY], preferred_element_type=F32)
            pr_out[g, d] = part.astype(BF16)
            pr_copy(g, d).start()
        own_part[g] = jnp.dot(both, wo_all[y], preferred_element_type=F32)

    def attend(step, unused):
        dz = digit(order_code([o[0] for o in ORDER]), step)
        j = digit(order_code([o[1] for o in ORDER]), step)
        r = digit(order_code([o[2] for o in ORDER]), step)
        block = 2 * ((x + j * to_next) % NX) + (zhi + dz) % 2

        for chunk in range(CHUNKS):
            @pl.when(step == STEP_FORWARD[chunk])
            def _():
                q_copy(0, 0, 0, chunk, 1, z_peer).wait_recv()
                q_copy(2, 1, 1, chunk, 1, x_peer(to_next)).start()

        @pl.when(step == STEP_KEYS)
        def _():
            kv_copy(0, 0, p, z_peer).start()

        @pl.when(step == LATE_FRESH)
        def _():
            for kind in range(2):
                kv_copy(kind, 1, px, z_peer).wait_recv()
            kfT[1] = kv_all[0, px].T
            vfa[1, :, pl.ds(0, HD)] = kv_all[1, px]

        @pl.when(j > 0)
        def _():
            q_copy(1, 0, 1, r, dz, z_peer).wait_recv()

        late = 1 - (step + len(ORDER) - LATE_FRESH) // len(ORDER)
        ahead = [
            offset + r * part_rows + (p_block - holder) * rows - far >= 0
            for p_block, holder, far in ((block, p, 0), (block, px, late * 2**20))
        ]

        query = q_all[dz, j, r]
        wide = jnp.concatenate([query, one_lane], 1)

        def score(side, at):
            scores = [jnp.dot(wide, kT[side, :, pl.ds(at, CHUNK)], preferred_element_type=F32)]
            if at + CHUNK == slots:
                fresh = jnp.dot(query, kfT[side], preferred_element_type=F32)
                scores.append(jnp.where(ahead[side], fresh, NEG))
            top = jnp.max(scores[0], -1, keepdims=True)
            for part in scores[1:]:
                top = jnp.maximum(top, jnp.max(part, -1, keepdims=True))
            return scores, top

        def weigh_values(side, at, scores, top):
            summed = None
            for part, value in zip(scores, (va[side, pl.ds(at, CHUNK), :], vfa[side])):
                weights = jnp.exp2(part - top).astype(BF16)
                term = jnp.dot(weights, value, preferred_element_type=F32)
                summed = term if summed is None else summed + term
            return summed, top

        pieces = [(side, at) for side in range(2) for at in range(0, slots, CHUNK)]
        current = score(*pieces[0])
        sums = []
        for number, piece in enumerate(pieces):
            following = score(*pieces[number + 1]) if number + 1 < len(pieces) else None
            sums.append(weigh_values(*piece, *current))
            current = following
        top = sums[0][1]
        for one, one_top in sums[1:]:
            top = jnp.maximum(top, one_top)
        summed = sums[0][0] * jnp.exp2(sums[0][1] - top)
        for one, one_top in sums[1:]:
            summed = summed + one * jnp.exp2(one_top - top)
        total = summed[:, HD:]
        o_buf[dz, j, r] = (summed[:, :HD] / total).astype(BF16)
        logsum = top + jnp.log(total) * LOG2E
        for hd in range(heads):
            l_buf[dz, j, r, pl.ds(hd, 1), :] = jnp.sum(
                jnp.where(eye, logsum[hd * part_rows:(hd + 1) * part_rows], 0.0), 0, keepdims=True
            )

        @pl.when(j > 0)
        def _():
            for copy in o_copies(dz, r):
                copy.start()

        for chunk in range(CHUNKS):
            @pl.when(step == STEP_MERGE[chunk])
            def _():
                merge_for_z(chunk)

        @pl.when(step == STEP_MERGE[-1])
        def _():
            kv_copy(1, 0, p, z_peer).start()

        @pl.when(step == STEP_BLEND)
        def _():
            attend_late_fresh()
            blend_group(0)

        @pl.when(step == STEP_PROJECT)
        def _():
            project_group(0)

        return unused

    lax.fori_loop(0, len(ORDER), attend, 0)

    others = (to_pair, to_next, 2)
    for kind in range(2):
        for k, d in ((2, to_next), (3, 2)):
            kv_copy(kind, k, p, x_peer(d)).start()

    def pass_on(kind):
        kv_copy(kind, 0, pz, z_peer).wait_recv()
        for k, d in enumerate(others):
            kv_copy(kind, 4 + k, pz, x_peer(d)).start()

    pass_on(0)
    blend_group(1)
    project_group(1)
    pass_on(1)

    for kind in range(2):
        for d in (to_next, 2):
            kv_copy(kind, 0, 2 * ((x + d) % NX) + zhi, z_peer).wait_recv()
        for d in others:
            kv_copy(kind, 0, 2 * ((x + d) % NX) + (zhi + 1) % 2, z_peer).wait_recv()
        for block in range(GROUP):
            fresh_pad[kind, pl.ds(slots + block * rows, rows), :] = kv_all[kind, block].astype(F32)
    start = p * slots - length
    begin = jnp.clip(start + slots, 0, 2 * slots)

    def place_rows(i, unused):
        at = pl.ds(pl.multiple_of(i * rows, rows), rows)
        token = start + i * rows + lax.broadcasted_iota(jnp.int32, (rows, HD), 0)
        written = jnp.logical_and(token >= 0, token < GROUP * rows)
        window = pl.ds(begin + i * rows, rows)
        for kind in range(2):
            cached = kraw[0, at, :] if kind == 0 else va[0, at, pl.ds(0, HD)]
            fresh = fresh_pad[kind, window, :].astype(BF16)
            updated[kind, at, :] = jnp.where(written, fresh, cached)
        return unused

    lax.fori_loop(0, GROUP, place_rows, 0)
    stores = [
        pltpu.make_async_copy(updated.at[0], keys_out, out_sem.at[0]),
        pltpu.make_async_copy(updated.at[1], values_out, out_sem.at[1]),
    ]
    for store in stores:
        store.start()

    for g in range(GROUPS):
        result = own_part[g]
        for d in (1, 3, 2):
            pr_copy(g, (NY - d) % NY).wait_recv()
        for d in (1, 2, 3):
            result = result + pr_in[g, d].astype(F32)
        out[pl.ds(g * (rows // GROUPS), rows // GROUPS), :] = result.astype(BF16)

    for k in range(3):
        ag_copy(k, h, s, sib, tok).wait_send()
    ag_copy(3, h, s, sib, tok).wait_send()
    for k in range(4, 7):
        ag_copy(k, h, s, sib).wait_send()
    for copy in wo_copies:
        copy.wait_send()
    for copy in pair_copies:
        copy.wait_send()
    for kind in range(2):
        for k in range(7):
            kv_copy(kind, k, p, z_peer).wait_send()
    for r in range(CHUNKS):
        for k in range(3):
            q_copy(k, 0, 0, r, 1, z_peer).wait_send()
        for copy in o_copies(0, r) + o_copies(1, r) + z_copies(r):
            copy.wait_send()
    for g in range(GROUPS):
        att_copy(g, c).wait_send()
        for d in (1, 2, 3):
            pr_copy(g, d).wait_send()
    for store in stores:
        store.wait()


def hand_on(*refs):
    sources, targets, held, (in_sem, out_sem) = refs[:3], refs[3:6], refs[6:9], refs[9:]
    pieces = []
    for at, source in enumerate(sources):
        share = source.shape[0] // 2
        pieces += [(at, half, pl.ds(half * share, share)) for half in range(2)]
    arriving = [
        pltpu.make_async_copy(sources[at].at[window], held[at].at[window], in_sem.at[at, half])
        for at, half, window in pieces
    ]
    leaving = [
        pltpu.make_async_copy(held[at].at[window], targets[at].at[window], out_sem.at[at, half])
        for at, half, window in pieces
    ]
    for copy in arriving:
        copy.start()
    for first, second in zip(arriving, leaving):
        first.wait()
        second.start()
    for copy in leaving:
        copy.wait()


def shards(
    tokens, norm_gain, w_query, w_key, w_value, w_out, keys_cache, values_cache,
    cached_lengths, rope_offsets,
):
    rows, width = tokens.shape
    slots = keys_cache.shape[0]
    heads = width // HD
    half = np.arange(HD) % (HD // 2)
    frequency = (ROPE_BASE ** (-half * 2.0 / HD)).astype(np.float32)[None]

    hbm_spec = pl.BlockSpec(memory_space=pltpu.HBM)
    vmem_spec = pl.BlockSpec(memory_space=pltpu.VMEM)
    smem_spec = pl.BlockSpec(memory_space=pltpu.SMEM)
    dma = pltpu.SemaphoreType.DMA
    block = (heads * rows // CHUNKS, HD)
    results = pl.pallas_call(
        kernel,
        out_shape=(
            jax.ShapeDtypeStruct((rows, width), BF16),
            jax.ShapeDtypeStruct((slots, HD), BF16),
            jax.ShapeDtypeStruct((slots, HD), BF16),
        ),
        in_specs=[hbm_spec] * 9 + [smem_spec] * 2,
        out_specs=(vmem_spec, hbm_spec, hbm_spec),
        scratch_shapes=[
            pltpu.VMEM((8, rows, width), BF16),
            pltpu.VMEM((8, 1, width), F32),
            pltpu.VMEM((1, HD), F32),
            pltpu.VMEM(w_query.shape, BF16),
            pltpu.VMEM(w_key.shape, BF16),
            pltpu.VMEM(w_value.shape, BF16),
            pltpu.VMEM((NY, 2 * width, width), BF16),
            pltpu.VMEM((2, slots, HD), BF16),
            pltpu.VMEM((2, 2 * HD, slots), BF16),
            pltpu.VMEM((2, slots, 2 * HD), BF16),
            pltpu.VMEM((2, HD, rows), BF16),
            pltpu.VMEM((2, rows, 2 * HD), BF16),
            pltpu.VMEM((rows, width + 2 * HD), F32),
            pltpu.VMEM((rows, HD), F32),
            pltpu.VMEM((rows, HD), F32),
            pltpu.VMEM((rows, HD), F32),
            pltpu.VMEM((2, 3 * slots, HD), F32),
            pltpu.VMEM((2, slots, HD), BF16),
            pltpu.VMEM((2, 2, CHUNKS) + block, BF16),
            pltpu.VMEM((2, GROUP, rows, HD), BF16),
            pltpu.VMEM((2, 2, CHUNKS) + block, BF16),
            pltpu.VMEM((2, 2, CHUNKS, 8, HD), F32),
            pltpu.VMEM((2, CHUNKS) + block, BF16),
            pltpu.VMEM((2, CHUNKS, 8, HD), F32),
            pltpu.VMEM((CHUNKS,) + block, BF16),
            pltpu.VMEM((CHUNKS, 8, HD), F32),
            pltpu.VMEM((CHUNKS,) + block, BF16),
            pltpu.VMEM((CHUNKS, 8, HD), F32),
            pltpu.VMEM((GROUPS, 2, rows // GROUPS, width), BF16),
            pltpu.VMEM((GROUPS, NY, rows // GROUPS, width), BF16),
            pltpu.VMEM((GROUPS, NY, rows // GROUPS, width), BF16),
            pltpu.VMEM((GROUPS, rows // GROUPS, width), F32),
            pltpu.VMEM((LATE_FRESH,) + block, BF16),
            pltpu.VMEM((LATE_FRESH, 8, HD), F32),
            dma((8,)), dma((NY,)), dma((7,)), dma((8,)), dma((NY,)), dma((NY,)), dma((2,)), dma((2,)),
            dma((3, CHUNKS)), dma((2, 2, CHUNKS)), dma((2, 7)), dma((2, GROUP)),
            dma((2, CHUNKS)), dma((2, CHUNKS)), dma((2, CHUNKS)), dma((2, CHUNKS)),
            dma((CHUNKS,)), dma((CHUNKS,)), dma((CHUNKS,)), dma((CHUNKS,)),
            dma((GROUPS,)), dma((GROUPS,)), dma((GROUPS, NY)), dma((GROUPS, NY)), dma((2,)),
        ],
        compiler_params=pltpu.CompilerParams(
            collective_id=0, has_side_effects=True, vmem_limit_bytes=64 << 20
        ),
        name="span_attention",
    )(
        tokens, norm_gain.reshape(8, 1, width), w_query, w_key, w_value, w_out,
        keys_cache, values_cache, frequency, cached_lengths, rope_offsets,
    )
    return pl.pallas_call(
        hand_on,
        out_shape=tuple(jax.ShapeDtypeStruct(one.shape, one.dtype) for one in results),
        in_specs=[hbm_spec] * 3,
        out_specs=(hbm_spec,) * 3,
        scratch_shapes=[pltpu.VMEM(one.shape, one.dtype) for one in results]
        + [dma((3, 2)), dma((3, 2))],
        name="hand_on",
    )(*results)


def solution(mesh):
    return jax.shard_map(
        shards,
        mesh=mesh,
        in_specs=(
            P("seq", "head"), P(), P(None, "head"), P(None, "head"), P(None, "head"),
            P("head", None), P("seq", "head"), P("seq", "head"), P(), P(),
        ),
        out_specs=(P("seq", "head"), P("seq", "head"), P("seq", "head")),
        check_vma=False,
    )
```

```python
import math

import jax
import jax.numpy as jnp
import numpy as np
from jax import lax
from jax.experimental import pallas as pl
from jax.experimental.pallas import tpu as pltpu
from jax.sharding import PartitionSpec as P

HD = 128
NX = 4
NZ = 8
NY = 4
GROUP = 8
NEG = -(2.0**100)
ROPE_BASE = 500000.0
EPS = 1e-05
LOG2E = 1.4426950408889634
F32 = jnp.float32
BF16 = jnp.bfloat16


def digit(number, place):
    value = number
    result = value % 10
    for at in range(1, 16):
        value = value // 10
        flag = (place + 16 - at) // 16 - (place + 15 - at) // 16
        result = result + flag * (value % 10 - number % 10)
    return result


def order_code(digits):
    return sum(d * 10**i for i, d in enumerate(digits))


ORDER = [(0, 0, 0), (0, 0, 1), (0, 1, 0), (1, 0, 0), (1, 1, 0), (1, 1, 1), (1, 0, 1), (0, 1, 1)]
LATE_FRESH = 2
STEP_FORWARD = (3, 4)
STEP_MERGE = (5, 6)
STEP_KEYS = 0
CHUNK = 2048
CHUNKS = 2
GROUPS = 2


def kernel(
    tok, gain, wq, wk, wv, wo, kc, vc, freq, lens, offs,
    out, keys_out, values_out,
    x_all, gain_v, freq_v, wq_v, wk_v, wv_v, wo_all, kraw, kT, va, kfT, vfa, acc, ssq,
    cos, sin, fresh_pad, updated, q_all, kv_all, o_buf, l_buf, o_in, l_in,
    oz_out, lz_out, oz_in, lz_in, att_all, pr_out, pr_in, own_part, late_o, late_l,
    load_sem, own_wo_sem, ag_send, ag_recv, wo_send, wo_recv, pair_send, pair_recv,
    q_send, q_recv, kv_send, kv_recv, o_send, o_recv, l_send, l_recv,
    z_send, z_recv, lz_send, lz_recv, att_send, att_recv, pr_send, pr_recv, out_sem,
):
    rows, width = tok.shape
    heads = width // HD
    slots = kc.shape[0]
    s = lax.axis_index("seq")
    h = lax.axis_index("head")
    x, z = s // NZ, s % NZ
    zhi = z // 4
    request = s % 4
    y, c = h // 2, h % 2
    p = s // 4
    z_peer = x * NZ + (z + 4) % NZ
    pz = z_peer // 4
    sib = y * 2 + (1 - c)
    odd = (x + c) % 2
    to_pair, to_next = 1 + 2 * odd, 3 - 2 * odd
    px = 2 * ((x + to_pair) % NX) + zhi
    part_rows = rows // CHUNKS

    def x_peer(d):
        return ((x + d) % NX) * NZ + z

    def y_peer(d):
        return ((y + d) % NY) * 2 + c

    def remote(src, dst, send, recv, seq, head):
        return pltpu.make_async_remote_copy(
            src_ref=src, dst_ref=dst, send_sem=send, recv_sem=recv,
            device_id=(seq, head), device_id_type=pl.DeviceIdType.MESH,
        )

    loads = [
        pltpu.make_async_copy(tok, x_all.at[h], load_sem.at[0]),
        pltpu.make_async_copy(wq, wq_v, load_sem.at[1]),
        pltpu.make_async_copy(wk, wk_v, load_sem.at[2]),
        pltpu.make_async_copy(wv, wv_v, load_sem.at[3]),
        pltpu.make_async_copy(kc, kraw.at[0], load_sem.at[4]),
        pltpu.make_async_copy(vc, va.at[0, :, pl.ds(0, HD)], load_sem.at[5]),
        pltpu.make_async_copy(gain, gain_v, load_sem.at[6]),
        pltpu.make_async_copy(freq, freq_v, load_sem.at[7]),
    ]
    loads[0].start()

    def wo_columns(yy, cc):
        return wo.at[:, pl.ds(pl.multiple_of((yy * 2 + cc) * width, width), width)]

    def wo_rows(yy, cc):
        return wo_all.at[yy, pl.ds(pl.multiple_of(cc * width, width), width), :]

    own_wo = [
        pltpu.make_async_copy(wo_columns(yy, c), wo_rows(yy, c), own_wo_sem.at[yy])
        for yy in range(NY)
    ]
    barrier = pltpu.get_barrier_semaphore()
    peers = [(s, sib), (z_peer, h)]
    peers += [(s, y_peer(d)) for d in (1, 2, 3)] + [(x_peer(d), h) for d in (1, 2, 3)]
    for seq, head in peers:
        pl.semaphore_signal(
            barrier, inc=1, device_id=(seq, head), device_id_type=pl.DeviceIdType.MESH
        )
    for kind in range(2):
        fresh_pad[kind, pl.ds(0, slots), :] = jnp.zeros((slots, HD), F32)
        fresh_pad[kind, pl.ds(2 * slots, slots), :] = jnp.zeros((slots, HD), F32)
    for side in range(2):
        va[side, :, pl.ds(HD, HD)] = jnp.ones((slots, HD), BF16)
        vfa[side, :, pl.ds(HD, HD)] = jnp.ones((rows, HD), BF16)
    acc[...] = jnp.zeros_like(acc)
    ssq[...] = jnp.zeros_like(ssq)
    l_buf[...] = jnp.zeros_like(l_buf)
    late_l[...] = jnp.zeros_like(late_l)
    pl.semaphore_wait(barrier, len(peers))

    def ag_copy(k, source, seq, head, src=None):
        return remote(
            x_all.at[source] if src is None else src, x_all.at[source],
            ag_send.at[k], ag_recv.at[source], seq, head,
        )

    for k, d in enumerate((2, 1, 3)):
        ag_copy(k, h, s, y_peer(d), tok).start()
    ag_copy(3, h, s, sib, tok).start()
    wo_copies = [
        remote(wo_columns(yy, 1 - c), wo_rows(yy, c), wo_send.at[yy], wo_recv.at[yy], s, sib)
        for yy in range(NY)
    ]
    pair_copies = [
        remote(kc, kraw.at[1], pair_send.at[0], pair_recv.at[0], x_peer(to_pair), h),
        remote(vc, va.at[1, :, pl.ds(0, HD)], pair_send.at[1], pair_recv.at[1], x_peer(to_pair), h),
    ]
    for copy in pair_copies:
        copy.start()
    for load in loads[1:] + own_wo:
        load.start()

    length = lens[request]

    def prepare_keys(side, holder):
        for at in range(0, slots, 512):
            kT[side, pl.ds(0, HD), pl.ds(at, 512)] = kraw[side, pl.ds(at, 512), :].T
        slot = holder * slots + lax.broadcasted_iota(jnp.int32, (HD, slots), 1)
        first_row = lax.broadcasted_iota(jnp.int32, (HD, slots), 0) == 0
        hidden = jnp.logical_and(first_row, slot >= length)
        kT[side, pl.ds(HD, HD), :] = jnp.where(hidden, NEG, 0.0).astype(BF16)

    loads[4].wait()
    loads[5].wait()
    prepare_keys(0, p)
    for at in (0, 1, 2, 3, 6, 7):
        loads[at].wait()
    place = offs[request] + length + p * rows
    place = place + lax.broadcasted_iota(jnp.int32, (rows, HD), 0)
    angles = place.astype(F32) * freq_v[...]
    sign = jnp.where(lax.broadcasted_iota(jnp.int32, (rows, HD), 1) < HD // 2, -1.0, 1.0)
    cos[...] = jnp.cos(angles)
    sin[...] = jnp.sin(angles) * sign

    def project(step, unused):
        d = digit(order_code([0, 0, 1, 3, 2, 1, 3, 2]), step)
        other = digit(order_code([0, 1, 0, 0, 0, 1, 1, 1]), step)
        source = ((y + d) % NY) * 2 + (c + other) % 2

        @pl.when(step > 0)
        def _():
            ag_copy(0, source, s, sib).wait_recv()

        @pl.when(jnp.logical_and(step >= 2, step < 5))
        def _():
            ag_copy(2 + step, source, s, sib).start()

        shard = x_all[source].astype(F32)
        square = shard * shard
        ssq[...] += square[:, :HD] + square[:, HD:2 * HD] + square[:, 2 * HD:]
        scaled = (shard * gain_v[source]).astype(BF16)
        at = pl.ds(pl.multiple_of(source * width, width), width)
        acc[:, pl.ds(0, width)] += jnp.dot(scaled, wq_v[at, :], preferred_element_type=F32)
        acc[:, pl.ds(width, HD)] += jnp.dot(scaled, wk_v[at, :], preferred_element_type=F32)
        acc[:, pl.ds(width + HD, HD)] += jnp.dot(scaled, wv_v[at, :], preferred_element_type=F32)
        return unused

    lax.fori_loop(0, 8, project, 0)

    scale = lax.rsqrt(jnp.sum(ssq[...], -1, keepdims=True) * (1.0 / (width * 8)) + EPS)
    cosine = cos[...]
    sine = sin[...]

    def rope(vectors):
        return vectors * cosine + pltpu.roll(vectors, HD // 2, 1) * sine

    def kv_copy(kind, k, block, seq):
        return remote(
            kv_all.at[kind, block], kv_all.at[kind, block],
            kv_send.at[kind, k], kv_recv.at[kind, block], seq, h,
        )

    fresh_key = rope(acc[:, pl.ds(width, HD)] * scale).astype(BF16)
    fresh_value = (acc[:, pl.ds(width + HD, HD)] * scale).astype(BF16)
    kv_all[0, p] = fresh_key
    kv_all[1, p] = fresh_value
    for kind in range(2):
        kv_copy(kind, 1, p, x_peer(to_pair)).start()

    def q_copy(k, dz, j, r, to_z, seq):
        return remote(
            q_all.at[dz, 0, r], q_all.at[to_z, j, r], q_send.at[k, r], q_recv.at[to_z, j, r], seq, h
        )

    fold = LOG2E / math.sqrt(HD)
    for r in range(CHUNKS):
        window = pl.ds(r * part_rows, part_rows)
        for hd in range(heads):
            vectors = acc[window, pl.ds(hd * HD, HD)] * scale[r * part_rows:(r + 1) * part_rows]
            turned = vectors * cos[window, :] + pltpu.roll(vectors, HD // 2, 1) * sin[window, :]
            q_all[0, 0, r, pl.ds(hd * part_rows, part_rows), :] = (turned * fold).astype(BF16)
        q_copy(0, 0, 0, r, 1, z_peer).start()
        q_copy(1, 0, 1, r, 0, x_peer(to_next)).start()
    for copy in wo_copies:
        copy.start()

    kfT[0] = fresh_key.T
    vfa[0, :, pl.ds(0, HD)] = fresh_value
    for copy in pair_copies:
        copy.wait_recv()
    prepare_keys(1, px)
    kfT[1] = jnp.zeros((HD, rows), BF16)
    vfa[1, :, pl.ds(0, HD)] = jnp.zeros((rows, HD), BF16)

    eye = lax.broadcasted_iota(jnp.int32, (part_rows, HD), 0) == lax.broadcasted_iota(
        jnp.int32, (part_rows, HD), 1
    )
    stacked = heads * part_rows
    first_lane = lax.broadcasted_iota(jnp.int32, (stacked, HD), 1) == 0
    one_lane = jnp.where(first_lane, 1.0, 0.0).astype(BF16)
    offset = lax.broadcasted_iota(jnp.int32, (stacked, rows), 0) % part_rows
    offset = offset - lax.broadcasted_iota(jnp.int32, (stacked, rows), 1)

    def o_copies(dz, r):
        return (
            remote(o_buf.at[dz, 1, r], o_in.at[dz, r], o_send.at[dz, r], o_recv.at[dz, r],
                   x_peer(to_next), h),
            remote(l_buf.at[dz, 1, r], l_in.at[dz, r], l_send.at[dz, r], l_recv.at[dz, r],
                   x_peer(to_next), h),
        )

    def z_copies(r):
        return (
            remote(oz_out.at[r], oz_in.at[r], z_send.at[r], z_recv.at[r], z_peer, h),
            remote(lz_out.at[r], lz_in.at[r], lz_send.at[r], lz_recv.at[r], z_peer, h),
        )

    def weigh(logsums):
        highest = logsums[0]
        for one in logsums[1:]:
            highest = jnp.maximum(highest, one)
        shares = [jnp.exp2(one - highest) for one in logsums]
        total = shares[0]
        for one in shares[1:]:
            total = total + one
        return [one / total for one in shares], highest + jnp.log(total) * LOG2E

    def blend(parts, shares, hd):
        result = None
        for part, share in zip(parts, shares):
            column = jnp.sum(jnp.where(eye, share[hd:hd + 1, :], 0.0), 1, keepdims=True)
            term = part[pl.ds(hd * part_rows, part_rows), :].astype(F32) * column
            result = term if result is None else result + term
        return result

    def merge_for_z(r):
        for copy in o_copies(1, r):
            copy.wait_recv()
        shares, merged = weigh([l_buf[1, 0, r], l_in[1, r]])
        lz_out[r] = merged
        for hd in range(heads):
            oz_out[r, pl.ds(hd * part_rows, part_rows), :] = blend(
                [o_buf.at[1, 0, r], o_in.at[1, r]], shares, hd
            ).astype(BF16)
        for copy in z_copies(r):
            copy.start()

    def att_copy(g, core):
        return remote(
            att_all.at[g, core], att_all.at[g, core], att_send.at[g], att_recv.at[g], s, sib
        )

    def pr_copy(g, d):
        back = (NY - d) % NY
        return remote(
            pr_out.at[g, d], pr_in.at[g, back], pr_send.at[g, d], pr_recv.at[g, back], s, y_peer(d)
        )

    def attend_late_fresh():
        for r in range(LATE_FRESH):
            scores = jnp.dot(q_all[0, 0, r], kfT[1], preferred_element_type=F32)
            scores = jnp.where(offset + r * part_rows + (p - px) * rows >= 0, scores, NEG)
            top = jnp.max(scores, -1, keepdims=True)
            weights = jnp.exp2(scores - top).astype(BF16)
            summed = jnp.dot(weights, vfa[1], preferred_element_type=F32)
            total = summed[:, HD:]
            late_o[r] = (summed[:, :HD] / total).astype(BF16)
            logsum = top + jnp.log(total) * LOG2E
            for hd in range(heads):
                late_l[r, pl.ds(hd, 1), :] = jnp.sum(
                    jnp.where(eye, logsum[hd * part_rows:(hd + 1) * part_rows], 0.0),
                    0, keepdims=True,
                )

    per_group = CHUNKS // GROUPS

    def blend_group(g):
        for k in range(per_group):
            r = g * per_group + k
            for copy in o_copies(0, r) + z_copies(r):
                copy.wait_recv()
            parts = [o_buf.at[0, 0, r], o_in.at[0, r], oz_in.at[r]]
            logsums = [l_buf[0, 0, r], l_in[0, r], lz_in[r]]
            if r < LATE_FRESH:
                parts.append(late_o.at[r])
                logsums.append(late_l[r])
            shares, merged = weigh(logsums)
            for hd in range(heads):
                att_all[g, c, pl.ds(k * part_rows, part_rows), pl.ds(hd * HD, HD)] = blend(
                    parts, shares, hd
                ).astype(BF16)
        att_copy(g, c).start()

    def project_group(g):
        if g == 0:
            for load in own_wo:
                load.wait()
            for copy in wo_copies:
                copy.wait_recv()
        att_copy(g, 1 - c).wait_recv()
        both = jnp.concatenate([att_all[g, 0], att_all[g, 1]], 1)
        for d in (2, 1, 3):
            part = jnp.dot(both, wo_all[(y + d) % NY], preferred_element_type=F32)
            pr_out[g, d] = part.astype(BF16)
            pr_copy(g, d).start()
        own_part[g] = jnp.dot(both, wo_all[y], preferred_element_type=F32)

    def attend(step, unused):
        dz = digit(order_code([o[0] for o in ORDER]), step)
        j = digit(order_code([o[1] for o in ORDER]), step)
        r = digit(order_code([o[2] for o in ORDER]), step)
        block = 2 * ((x + j * to_next) % NX) + (zhi + dz) % 2

        for chunk in range(CHUNKS):
            @pl.when(step == STEP_FORWARD[chunk])
            def _():
                q_copy(0, 0, 0, chunk, 1, z_peer).wait_recv()
                q_copy(2, 1, 1, chunk, 1, x_peer(to_next)).start()

        @pl.when(step == STEP_KEYS)
        def _():
            for kind in range(2):
                kv_copy(kind, 0, p, z_peer).start()

        @pl.when(step == LATE_FRESH)
        def _():
            for kind in range(2):
                kv_copy(kind, 1, px, z_peer).wait_recv()
            kfT[1] = kv_all[0, px].T
            vfa[1, :, pl.ds(0, HD)] = kv_all[1, px]

        @pl.when(j > 0)
        def _():
            q_copy(1, 0, 1, r, dz, z_peer).wait_recv()

        late = 1 - (step + len(ORDER) - LATE_FRESH) // len(ORDER)
        ahead = [
            offset + r * part_rows + (p_block - holder) * rows - far >= 0
            for p_block, holder, far in ((block, p, 0), (block, px, late * 2**20))
        ]

        query = q_all[dz, j, r]
        wide = jnp.concatenate([query, one_lane], 1)

        def score(side, at):
            scores = [jnp.dot(wide, kT[side, :, pl.ds(at, CHUNK)], preferred_element_type=F32)]
            if at + CHUNK == slots:
                fresh = jnp.dot(query, kfT[side], preferred_element_type=F32)
                scores.append(jnp.where(ahead[side], fresh, NEG))
            top = jnp.max(scores[0], -1, keepdims=True)
            for part in scores[1:]:
                top = jnp.maximum(top, jnp.max(part, -1, keepdims=True))
            return scores, top

        def weigh_values(side, at, scores, top):
            summed = None
            for part, value in zip(scores, (va[side, pl.ds(at, CHUNK), :], vfa[side])):
                weights = jnp.exp2(part - top).astype(BF16)
                term = jnp.dot(weights, value, preferred_element_type=F32)
                summed = term if summed is None else summed + term
            return summed, top

        pieces = [(side, at) for side in range(2) for at in range(0, slots, CHUNK)]
        current = score(*pieces[0])
        sums = []
        for number, piece in enumerate(pieces):
            following = score(*pieces[number + 1]) if number + 1 < len(pieces) else None
            sums.append(weigh_values(*piece, *current))
            current = following
        top = sums[0][1]
        for one, one_top in sums[1:]:
            top = jnp.maximum(top, one_top)
        summed = sums[0][0] * jnp.exp2(sums[0][1] - top)
        for one, one_top in sums[1:]:
            summed = summed + one * jnp.exp2(one_top - top)
        total = summed[:, HD:]
        o_buf[dz, j, r] = (summed[:, :HD] / total).astype(BF16)
        logsum = top + jnp.log(total) * LOG2E
        for hd in range(heads):
            l_buf[dz, j, r, pl.ds(hd, 1), :] = jnp.sum(
                jnp.where(eye, logsum[hd * part_rows:(hd + 1) * part_rows], 0.0), 0, keepdims=True
            )

        @pl.when(j > 0)
        def _():
            for copy in o_copies(dz, r):
                copy.start()

        for chunk in range(CHUNKS):
            @pl.when(step == STEP_MERGE[chunk])
            def _():
                merge_for_z(chunk)

        return unused

    lax.fori_loop(0, len(ORDER), attend, 0)

    others = (to_pair, to_next, 2)
    for kind in range(2):
        for k, d in ((2, to_next), (3, 2)):
            kv_copy(kind, k, p, x_peer(d)).start()

    def pass_on(kind):
        kv_copy(kind, 0, pz, z_peer).wait_recv()
        for k, d in enumerate(others):
            kv_copy(kind, 4 + k, pz, x_peer(d)).start()

    pass_on(0)
    pass_on(1)
    attend_late_fresh()
    for g in range(GROUPS):
        blend_group(g)
        project_group(g)

    for kind in range(2):
        for d in (to_next, 2):
            kv_copy(kind, 0, 2 * ((x + d) % NX) + zhi, z_peer).wait_recv()
        for d in others:
            kv_copy(kind, 0, 2 * ((x + d) % NX) + (zhi + 1) % 2, z_peer).wait_recv()
        for block in range(GROUP):
            fresh_pad[kind, pl.ds(slots + block * rows, rows), :] = kv_all[kind, block].astype(F32)
    start = p * slots - length
    begin = jnp.clip(start + slots, 0, 2 * slots)

    def place_rows(i, unused):
        at = pl.ds(pl.multiple_of(i * rows, rows), rows)
        token = start + i * rows + lax.broadcasted_iota(jnp.int32, (rows, HD), 0)
        written = jnp.logical_and(token >= 0, token < GROUP * rows)
        window = pl.ds(begin + i * rows, rows)
        for kind in range(2):
            cached = kraw[0, at, :] if kind == 0 else va[0, at, pl.ds(0, HD)]
            fresh = fresh_pad[kind, window, :].astype(BF16)
            updated[kind, at, :] = jnp.where(written, fresh, cached)
        return unused

    lax.fori_loop(0, GROUP, place_rows, 0)
    stores = [
        pltpu.make_async_copy(updated.at[0], keys_out, out_sem.at[0]),
        pltpu.make_async_copy(updated.at[1], values_out, out_sem.at[1]),
    ]
    for store in stores:
        store.start()

    for g in range(GROUPS):
        result = own_part[g]
        for d in (1, 3, 2):
            pr_copy(g, (NY - d) % NY).wait_recv()
        for d in (1, 2, 3):
            result = result + pr_in[g, d].astype(F32)
        out[pl.ds(g * (rows // GROUPS), rows // GROUPS), :] = result.astype(BF16)

    for k in range(3):
        ag_copy(k, h, s, sib, tok).wait_send()
    ag_copy(3, h, s, sib, tok).wait_send()
    for k in range(4, 7):
        ag_copy(k, h, s, sib).wait_send()
    for copy in wo_copies:
        copy.wait_send()
    for copy in pair_copies:
        copy.wait_send()
    for kind in range(2):
        for k in range(7):
            kv_copy(kind, k, p, z_peer).wait_send()
    for r in range(CHUNKS):
        for k in range(3):
            q_copy(k, 0, 0, r, 1, z_peer).wait_send()
        for copy in o_copies(0, r) + o_copies(1, r) + z_copies(r):
            copy.wait_send()
    for g in range(GROUPS):
        att_copy(g, c).wait_send()
        for d in (1, 2, 3):
            pr_copy(g, d).wait_send()
    for store in stores:
        store.wait()


def hand_on(*refs):
    sources, targets, held, (in_sem, out_sem) = refs[:3], refs[3:6], refs[6:9], refs[9:]
    pieces = []
    for at, source in enumerate(sources):
        share = source.shape[0] // 2
        pieces += [(at, half, pl.ds(half * share, share)) for half in range(2)]
    arriving = [
        pltpu.make_async_copy(sources[at].at[window], held[at].at[window], in_sem.at[at, half])
        for at, half, window in pieces
    ]
    leaving = [
        pltpu.make_async_copy(held[at].at[window], targets[at].at[window], out_sem.at[at, half])
        for at, half, window in pieces
    ]
    for copy in arriving:
        copy.start()
    for first, second in zip(arriving, leaving):
        first.wait()
        second.start()
    for copy in leaving:
        copy.wait()


def shards(
    tokens, norm_gain, w_query, w_key, w_value, w_out, keys_cache, values_cache,
    cached_lengths, rope_offsets,
):
    rows, width = tokens.shape
    slots = keys_cache.shape[0]
    heads = width // HD
    half = np.arange(HD) % (HD // 2)
    frequency = (ROPE_BASE ** (-half * 2.0 / HD)).astype(np.float32)[None]

    hbm_spec = pl.BlockSpec(memory_space=pltpu.HBM)
    vmem_spec = pl.BlockSpec(memory_space=pltpu.VMEM)
    smem_spec = pl.BlockSpec(memory_space=pltpu.SMEM)
    dma = pltpu.SemaphoreType.DMA
    block = (heads * rows // CHUNKS, HD)
    results = pl.pallas_call(
        kernel,
        out_shape=(
            jax.ShapeDtypeStruct((rows, width), BF16),
            jax.ShapeDtypeStruct((slots, HD), BF16),
            jax.ShapeDtypeStruct((slots, HD), BF16),
        ),
        in_specs=[hbm_spec] * 9 + [smem_spec] * 2,
        out_specs=(vmem_spec, hbm_spec, hbm_spec),
        scratch_shapes=[
            pltpu.VMEM((8, rows, width), BF16),
            pltpu.VMEM((8, 1, width), F32),
            pltpu.VMEM((1, HD), F32),
            pltpu.VMEM(w_query.shape, BF16),
            pltpu.VMEM(w_key.shape, BF16),
            pltpu.VMEM(w_value.shape, BF16),
            pltpu.VMEM((NY, 2 * width, width), BF16),
            pltpu.VMEM((2, slots, HD), BF16),
            pltpu.VMEM((2, 2 * HD, slots), BF16),
            pltpu.VMEM((2, slots, 2 * HD), BF16),
            pltpu.VMEM((2, HD, rows), BF16),
            pltpu.VMEM((2, rows, 2 * HD), BF16),
            pltpu.VMEM((rows, width + 2 * HD), F32),
            pltpu.VMEM((rows, HD), F32),
            pltpu.VMEM((rows, HD), F32),
            pltpu.VMEM((rows, HD), F32),
            pltpu.VMEM((2, 3 * slots, HD), F32),
            pltpu.VMEM((2, slots, HD), BF16),
            pltpu.VMEM((2, 2, CHUNKS) + block, BF16),
            pltpu.VMEM((2, GROUP, rows, HD), BF16),
            pltpu.VMEM((2, 2, CHUNKS) + block, BF16),
            pltpu.VMEM((2, 2, CHUNKS, 8, HD), F32),
            pltpu.VMEM((2, CHUNKS) + block, BF16),
            pltpu.VMEM((2, CHUNKS, 8, HD), F32),
            pltpu.VMEM((CHUNKS,) + block, BF16),
            pltpu.VMEM((CHUNKS, 8, HD), F32),
            pltpu.VMEM((CHUNKS,) + block, BF16),
            pltpu.VMEM((CHUNKS, 8, HD), F32),
            pltpu.VMEM((GROUPS, 2, rows // GROUPS, width), BF16),
            pltpu.VMEM((GROUPS, NY, rows // GROUPS, width), BF16),
            pltpu.VMEM((GROUPS, NY, rows // GROUPS, width), BF16),
            pltpu.VMEM((GROUPS, rows // GROUPS, width), F32),
            pltpu.VMEM((LATE_FRESH,) + block, BF16),
            pltpu.VMEM((LATE_FRESH, 8, HD), F32),
            dma((8,)), dma((NY,)), dma((7,)), dma((8,)), dma((NY,)), dma((NY,)), dma((2,)), dma((2,)),
            dma((3, CHUNKS)), dma((2, 2, CHUNKS)), dma((2, 7)), dma((2, GROUP)),
            dma((2, CHUNKS)), dma((2, CHUNKS)), dma((2, CHUNKS)), dma((2, CHUNKS)),
            dma((CHUNKS,)), dma((CHUNKS,)), dma((CHUNKS,)), dma((CHUNKS,)),
            dma((GROUPS,)), dma((GROUPS,)), dma((GROUPS, NY)), dma((GROUPS, NY)), dma((2,)),
        ],
        compiler_params=pltpu.CompilerParams(
            collective_id=0, has_side_effects=True, vmem_limit_bytes=64 << 20
        ),
        name="span_attention",
    )(
        tokens, norm_gain.reshape(8, 1, width), w_query, w_key, w_value, w_out,
        keys_cache, values_cache, frequency, cached_lengths, rope_offsets,
    )
    return pl.pallas_call(
        hand_on,
        out_shape=tuple(jax.ShapeDtypeStruct(one.shape, one.dtype) for one in results),
        in_specs=[hbm_spec] * 3,
        out_specs=(hbm_spec,) * 3,
        scratch_shapes=[pltpu.VMEM(one.shape, one.dtype) for one in results]
        + [dma((3, 2)), dma((3, 2))],
        name="hand_on",
    )(*results)


def solution(mesh):
    return jax.shard_map(
        shards,
        mesh=mesh,
        in_specs=(
            P("seq", "head"), P(), P(None, "head"), P(None, "head"), P(None, "head"),
            P("head", None), P("seq", "head"), P("seq", "head"), P(), P(),
        ),
        out_specs=(P("seq", "head"), P("seq", "head"), P("seq", "head")),
        check_vma=False,
    )
```

```python
import math

import jax
import jax.numpy as jnp
import numpy as np
from jax import lax
from jax.experimental import pallas as pl
from jax.experimental.pallas import tpu as pltpu
from jax.sharding import PartitionSpec as P

HD = 128
NX = 4
NZ = 8
NY = 4
GROUP = 8
NEG = -(2.0**100)
ROPE_BASE = 500000.0
EPS = 1e-05
LOG2E = 1.4426950408889634
F32 = jnp.float32
BF16 = jnp.bfloat16


def digit(number, place):
    value = number
    result = value % 10
    for at in range(1, 16):
        value = value // 10
        flag = (place + 16 - at) // 16 - (place + 15 - at) // 16
        result = result + flag * (value % 10 - number % 10)
    return result


def order_code(digits):
    return sum(d * 10**i for i, d in enumerate(digits))


ORDER = [(0, 0, 0), (0, 0, 1), (0, 1, 0), (1, 0, 0), (1, 1, 0), (1, 1, 1), (1, 0, 1), (0, 1, 1)]
LATE_FRESH = 2
STEP_FORWARD = (3, 4)
STEP_MERGE = (5, 6)
STEP_KEYS = 4
CHUNK = 2048
CHUNKS = 2
GROUPS = 2


def kernel(
    tok, gain, wq, wk, wv, wo, kc, vc, freq, lens, offs,
    out, keys_out, values_out,
    x_all, gain_v, freq_v, wq_v, wk_v, wv_v, wo_all, kraw, kT, va, kfT, vfa, acc, ssq,
    cos, sin, fresh_pad, updated, q_all, kv_all, o_buf, l_buf, o_in, l_in,
    oz_out, lz_out, oz_in, lz_in, att_all, pr_out, pr_in, own_part, late_o, late_l,
    load_sem, own_wo_sem, ag_send, ag_recv, wo_send, wo_recv, pair_send, pair_recv,
    q_send, q_recv, kv_send, kv_recv, o_send, o_recv, l_send, l_recv,
    z_send, z_recv, lz_send, lz_recv, att_send, att_recv, pr_send, pr_recv, out_sem,
):
    rows, width = tok.shape
    heads = width // HD
    slots = kc.shape[0]
    s = lax.axis_index("seq")
    h = lax.axis_index("head")
    x, z = s // NZ, s % NZ
    zhi = z // 4
    request = s % 4
    y, c = h // 2, h % 2
    p = s // 4
    z_peer = x * NZ + (z + 4) % NZ
    pz = z_peer // 4
    sib = y * 2 + (1 - c)
    odd = (x + c) % 2
    to_pair, to_next = 1 + 2 * odd, 3 - 2 * odd
    px = 2 * ((x + to_pair) % NX) + zhi
    part_rows = rows // CHUNKS

    def x_peer(d):
        return ((x + d) % NX) * NZ + z

    def y_peer(d):
        return ((y + d) % NY) * 2 + c

    def remote(src, dst, send, recv, seq, head):
        return pltpu.make_async_remote_copy(
            src_ref=src, dst_ref=dst, send_sem=send, recv_sem=recv,
            device_id=(seq, head), device_id_type=pl.DeviceIdType.MESH,
        )

    loads = [
        pltpu.make_async_copy(tok, x_all.at[h], load_sem.at[0]),
        pltpu.make_async_copy(wq, wq_v, load_sem.at[1]),
        pltpu.make_async_copy(wk, wk_v, load_sem.at[2]),
        pltpu.make_async_copy(wv, wv_v, load_sem.at[3]),
        pltpu.make_async_copy(kc, kraw.at[0], load_sem.at[4]),
        pltpu.make_async_copy(vc, va.at[0, :, pl.ds(0, HD)], load_sem.at[5]),
        pltpu.make_async_copy(gain, gain_v, load_sem.at[6]),
        pltpu.make_async_copy(freq, freq_v, load_sem.at[7]),
    ]
    loads[0].start()

    def wo_columns(yy, cc):
        return wo.at[:, pl.ds(pl.multiple_of((yy * 2 + cc) * width, width), width)]

    def wo_rows(yy, cc):
        return wo_all.at[yy, pl.ds(pl.multiple_of(cc * width, width), width), :]

    own_wo = [
        pltpu.make_async_copy(wo_columns(yy, c), wo_rows(yy, c), own_wo_sem.at[yy])
        for yy in range(NY)
    ]
    barrier = pltpu.get_barrier_semaphore()
    peers = [(z_peer, h), (s, y_peer(2)), (x_peer(2), h)]
    peers += [(s, y_peer(d)) for d in (1, 3)] + [(x_peer(d), h) for d in (1, 3)] + [(s, sib)]
    for seq, head in peers:
        pl.semaphore_signal(
            barrier, inc=1, device_id=(seq, head), device_id_type=pl.DeviceIdType.MESH
        )
    for kind in range(2):
        fresh_pad[kind, pl.ds(0, slots), :] = jnp.zeros((slots, HD), F32)
        fresh_pad[kind, pl.ds(2 * slots, slots), :] = jnp.zeros((slots, HD), F32)
    for side in range(2):
        va[side, :, pl.ds(HD, HD)] = jnp.ones((slots, HD), BF16)
        vfa[side, :, pl.ds(HD, HD)] = jnp.ones((rows, HD), BF16)
    acc[...] = jnp.zeros_like(acc)
    ssq[...] = jnp.zeros_like(ssq)
    l_buf[...] = jnp.zeros_like(l_buf)
    late_l[...] = jnp.zeros_like(late_l)
    pl.semaphore_wait(barrier, len(peers))

    def ag_copy(k, source, seq, head, src=None):
        return remote(
            x_all.at[source] if src is None else src, x_all.at[source],
            ag_send.at[k], ag_recv.at[source], seq, head,
        )

    for k, d in enumerate((2, 1, 3)):
        ag_copy(k, h, s, y_peer(d), tok).start()
    ag_copy(3, h, s, sib, tok).start()
    wo_copies = [
        remote(wo_columns(yy, 1 - c), wo_rows(yy, c), wo_send.at[yy], wo_recv.at[yy], s, sib)
        for yy in range(NY)
    ]
    pair_copies = [
        remote(kc, kraw.at[1], pair_send.at[0], pair_recv.at[0], x_peer(to_pair), h),
        remote(vc, va.at[1, :, pl.ds(0, HD)], pair_send.at[1], pair_recv.at[1], x_peer(to_pair), h),
    ]
    for copy in pair_copies:
        copy.start()
    for load in loads[1:] + own_wo:
        load.start()

    length = lens[request]

    def prepare_keys(side, holder):
        for at in range(0, slots, 512):
            kT[side, pl.ds(0, HD), pl.ds(at, 512)] = kraw[side, pl.ds(at, 512), :].T
        slot = holder * slots + lax.broadcasted_iota(jnp.int32, (HD, slots), 1)
        first_row = lax.broadcasted_iota(jnp.int32, (HD, slots), 0) == 0
        hidden = jnp.logical_and(first_row, slot >= length)
        kT[side, pl.ds(HD, HD), :] = jnp.where(hidden, NEG, 0.0).astype(BF16)

    loads[4].wait()
    loads[5].wait()
    prepare_keys(0, p)
    for at in (0, 1, 2, 3, 6, 7):
        loads[at].wait()
    place = offs[request] + length + p * rows
    place = place + lax.broadcasted_iota(jnp.int32, (rows, HD), 0)
    angles = place.astype(F32) * freq_v[...]
    sign = jnp.where(lax.broadcasted_iota(jnp.int32, (rows, HD), 1) < HD // 2, -1.0, 1.0)
    cos[...] = jnp.cos(angles)
    sin[...] = jnp.sin(angles) * sign

    def project(step, unused):
        d = digit(order_code([0, 0, 1, 3, 2, 1, 3, 2]), step)
        other = digit(order_code([0, 1, 0, 0, 0, 1, 1, 1]), step)
        source = ((y + d) % NY) * 2 + (c + other) % 2

        @pl.when(step > 0)
        def _():
            ag_copy(0, source, s, sib).wait_recv()

        @pl.when(jnp.logical_and(step >= 2, step < 5))
        def _():
            ag_copy(2 + step, source, s, sib).start()

        shard = x_all[source].astype(F32)
        square = shard * shard
        ssq[...] += square[:, :HD] + square[:, HD:2 * HD] + square[:, 2 * HD:]
        scaled = (shard * gain_v[source]).astype(BF16)
        at = pl.ds(pl.multiple_of(source * width, width), width)
        acc[:, pl.ds(0, width)] += jnp.dot(scaled, wq_v[at, :], preferred_element_type=F32)
        acc[:, pl.ds(width, HD)] += jnp.dot(scaled, wk_v[at, :], preferred_element_type=F32)
        acc[:, pl.ds(width + HD, HD)] += jnp.dot(scaled, wv_v[at, :], preferred_element_type=F32)
        return unused

    lax.fori_loop(0, 8, project, 0)

    scale = lax.rsqrt(jnp.sum(ssq[...], -1, keepdims=True) * (1.0 / (width * 8)) + EPS)
    cosine = cos[...]
    sine = sin[...]

    def rope(vectors):
        return vectors * cosine + pltpu.roll(vectors, HD // 2, 1) * sine

    def kv_copy(kind, k, block, seq):
        return remote(
            kv_all.at[kind, block], kv_all.at[kind, block],
            kv_send.at[kind, k], kv_recv.at[kind, block], seq, h,
        )

    def q_copy(k, dz, j, r, to_z, seq):
        return remote(
            q_all.at[dz, 0, r], q_all.at[to_z, j, r], q_send.at[k, r], q_recv.at[to_z, j, r], seq, h
        )

    fold = LOG2E / math.sqrt(HD)
    for r in range(CHUNKS):
        window = pl.ds(r * part_rows, part_rows)
        for hd in range(heads):
            vectors = acc[window, pl.ds(hd * HD, HD)] * scale[r * part_rows:(r + 1) * part_rows]
            turned = vectors * cos[window, :] + pltpu.roll(vectors, HD // 2, 1) * sin[window, :]
            q_all[0, 0, r, pl.ds(hd * part_rows, part_rows), :] = (turned * fold).astype(BF16)
        q_copy(0, 0, 0, r, 1, z_peer).start()
        q_copy(1, 0, 1, r, 0, x_peer(to_next)).start()
    fresh_key = rope(acc[:, pl.ds(width, HD)] * scale).astype(BF16)
    fresh_value = (acc[:, pl.ds(width + HD, HD)] * scale).astype(BF16)
    kv_all[0, p] = fresh_key
    kv_all[1, p] = fresh_value
    for kind in range(2):
        kv_copy(kind, 1, p, x_peer(to_pair)).start()
    for copy in wo_copies:
        copy.start()

    kfT[0] = fresh_key.T
    vfa[0, :, pl.ds(0, HD)] = fresh_value
    for copy in pair_copies:
        copy.wait_recv()
    prepare_keys(1, px)
    kfT[1] = jnp.zeros((HD, rows), BF16)
    vfa[1, :, pl.ds(0, HD)] = jnp.zeros((rows, HD), BF16)

    eye = lax.broadcasted_iota(jnp.int32, (part_rows, HD), 0) == lax.broadcasted_iota(
        jnp.int32, (part_rows, HD), 1
    )
    stacked = heads * part_rows
    first_lane = lax.broadcasted_iota(jnp.int32, (stacked, HD), 1) == 0
    one_lane = jnp.where(first_lane, 1.0, 0.0).astype(BF16)
    offset = lax.broadcasted_iota(jnp.int32, (stacked, rows), 0) % part_rows
    offset = offset - lax.broadcasted_iota(jnp.int32, (stacked, rows), 1)

    def o_copies(dz, r):
        return (
            remote(o_buf.at[dz, 1, r], o_in.at[dz, r], o_send.at[dz, r], o_recv.at[dz, r],
                   x_peer(to_next), h),
            remote(l_buf.at[dz, 1, r], l_in.at[dz, r], l_send.at[dz, r], l_recv.at[dz, r],
                   x_peer(to_next), h),
        )

    def z_copies(r):
        return (
            remote(oz_out.at[r], oz_in.at[r], z_send.at[r], z_recv.at[r], z_peer, h),
            remote(lz_out.at[r], lz_in.at[r], lz_send.at[r], lz_recv.at[r], z_peer, h),
        )

    def weigh(logsums):
        highest = logsums[0]
        for one in logsums[1:]:
            highest = jnp.maximum(highest, one)
        shares = [jnp.exp2(one - highest) for one in logsums]
        total = shares[0]
        for one in shares[1:]:
            total = total + one
        return [one / total for one in shares], highest + jnp.log(total) * LOG2E

    def blend(parts, shares, hd):
        result = None
        for part, share in zip(parts, shares):
            column = jnp.sum(jnp.where(eye, share[hd:hd + 1, :], 0.0), 1, keepdims=True)
            term = part[pl.ds(hd * part_rows, part_rows), :].astype(F32) * column
            result = term if result is None else result + term
        return result

    def merge_for_z(r):
        for copy in o_copies(1, r):
            copy.wait_recv()
        shares, merged = weigh([l_buf[1, 0, r], l_in[1, r]])
        lz_out[r] = merged
        for hd in range(heads):
            oz_out[r, pl.ds(hd * part_rows, part_rows), :] = blend(
                [o_buf.at[1, 0, r], o_in.at[1, r]], shares, hd
            ).astype(BF16)
        for copy in z_copies(r):
            copy.start()

    def att_copy(g, core):
        return remote(
            att_all.at[g, core], att_all.at[g, core], att_send.at[g], att_recv.at[g], s, sib
        )

    def pr_copy(g, d):
        back = (NY - d) % NY
        return remote(
            pr_out.at[g, d], pr_in.at[g, back], pr_send.at[g, d], pr_recv.at[g, back], s, y_peer(d)
        )

    def attend_late_fresh():
        for r in range(LATE_FRESH):
            scores = jnp.dot(q_all[0, 0, r], kfT[1], preferred_element_type=F32)
            scores = jnp.where(offset + r * part_rows + (p - px) * rows >= 0, scores, NEG)
            top = jnp.max(scores, -1, keepdims=True)
            weights = jnp.exp2(scores - top).astype(BF16)
            summed = jnp.dot(weights, vfa[1], preferred_element_type=F32)
            total = summed[:, HD:]
            late_o[r] = (summed[:, :HD] / total).astype(BF16)
            logsum = top + jnp.log(total) * LOG2E
            for hd in range(heads):
                late_l[r, pl.ds(hd, 1), :] = jnp.sum(
                    jnp.where(eye, logsum[hd * part_rows:(hd + 1) * part_rows], 0.0),
                    0, keepdims=True,
                )

    per_group = CHUNKS // GROUPS

    def blend_group(g):
        for k in range(per_group):
            r = g * per_group + k
            for copy in o_copies(0, r) + z_copies(r):
                copy.wait_recv()
            parts = [o_buf.at[0, 0, r], o_in.at[0, r], oz_in.at[r]]
            logsums = [l_buf[0, 0, r], l_in[0, r], lz_in[r]]
            if r < LATE_FRESH:
                parts.append(late_o.at[r])
                logsums.append(late_l[r])
            shares, merged = weigh(logsums)
            for hd in range(heads):
                att_all[g, c, pl.ds(k * part_rows, part_rows), pl.ds(hd * HD, HD)] = blend(
                    parts, shares, hd
                ).astype(BF16)
        att_copy(g, c).start()

    def project_group(g):
        if g == 0:
            for load in own_wo:
                load.wait()
            for copy in wo_copies:
                copy.wait_recv()
        att_copy(g, 1 - c).wait_recv()
        both = jnp.concatenate([att_all[g, 0], att_all[g, 1]], 1)
        for d in (2, 1, 3):
            part = jnp.dot(both, wo_all[(y + d) % NY], preferred_element_type=F32)
            pr_out[g, d] = part.astype(BF16)
            pr_copy(g, d).start()
        own_part[g] = jnp.dot(both, wo_all[y], preferred_element_type=F32)

    def attend(step, unused):
        dz = digit(order_code([o[0] for o in ORDER]), step)
        j = digit(order_code([o[1] for o in ORDER]), step)
        r = digit(order_code([o[2] for o in ORDER]), step)
        block = 2 * ((x + j * to_next) % NX) + (zhi + dz) % 2

        for chunk in range(CHUNKS):
            @pl.when(step == STEP_FORWARD[chunk])
            def _():
                q_copy(0, 0, 0, chunk, 1, z_peer).wait_recv()
                q_copy(2, 1, 1, chunk, 1, x_peer(to_next)).start()

        @pl.when(step == STEP_KEYS)
        def _():
            for kind in range(2):
                kv_copy(kind, 0, p, z_peer).start()

        @pl.when(step == LATE_FRESH)
        def _():
            for kind in range(2):
                kv_copy(kind, 1, px, z_peer).wait_recv()
            kfT[1] = kv_all[0, px].T
            vfa[1, :, pl.ds(0, HD)] = kv_all[1, px]

        @pl.when(j > 0)
        def _():
            q_copy(1, 0, 1, r, dz, z_peer).wait_recv()

        late = 1 - (step + len(ORDER) - LATE_FRESH) // len(ORDER)
        ahead = [
            offset + r * part_rows + (p_block - holder) * rows - far >= 0
            for p_block, holder, far in ((block, p, 0), (block, px, late * 2**20))
        ]

        query = q_all[dz, j, r]
        wide = jnp.concatenate([query, one_lane], 1)

        def score(side, at):
            scores = [jnp.dot(wide, kT[side, :, pl.ds(at, CHUNK)], preferred_element_type=F32)]
            if at + CHUNK == slots:
                fresh = jnp.dot(query, kfT[side], preferred_element_type=F32)
                scores.append(jnp.where(ahead[side], fresh, NEG))
            top = jnp.max(scores[0], -1, keepdims=True)
            for part in scores[1:]:
                top = jnp.maximum(top, jnp.max(part, -1, keepdims=True))
            return scores, top

        def weigh_values(side, at, scores, top):
            summed = None
            for part, value in zip(scores, (va[side, pl.ds(at, CHUNK), :], vfa[side])):
                weights = jnp.exp2(part - top).astype(BF16)
                term = jnp.dot(weights, value, preferred_element_type=F32)
                summed = term if summed is None else summed + term
            return summed, top

        pieces = [(side, at) for side in range(2) for at in range(0, slots, CHUNK)]
        current = score(*pieces[0])
        sums = []
        for number, piece in enumerate(pieces):
            following = score(*pieces[number + 1]) if number + 1 < len(pieces) else None
            sums.append(weigh_values(*piece, *current))
            current = following
        top = sums[0][1]
        for one, one_top in sums[1:]:
            top = jnp.maximum(top, one_top)
        summed = sums[0][0] * jnp.exp2(sums[0][1] - top)
        for one, one_top in sums[1:]:
            summed = summed + one * jnp.exp2(one_top - top)
        total = summed[:, HD:]
        o_buf[dz, j, r] = (summed[:, :HD] / total).astype(BF16)
        logsum = top + jnp.log(total) * LOG2E
        for hd in range(heads):
            l_buf[dz, j, r, pl.ds(hd, 1), :] = jnp.sum(
                jnp.where(eye, logsum[hd * part_rows:(hd + 1) * part_rows], 0.0), 0, keepdims=True
            )

        @pl.when(j > 0)
        def _():
            for copy in o_copies(dz, r):
                copy.start()

        for chunk in range(CHUNKS):
            @pl.when(step == STEP_MERGE[chunk])
            def _():
                merge_for_z(chunk)

        return unused

    lax.fori_loop(0, len(ORDER), attend, 0)

    others = (to_pair, to_next, 2)
    for kind in range(2):
        for k, d in ((2, to_next), (3, 2)):
            kv_copy(kind, k, p, x_peer(d)).start()

    def pass_on(kind):
        kv_copy(kind, 0, pz, z_peer).wait_recv()
        for k, d in enumerate(others):
            kv_copy(kind, 4 + k, pz, x_peer(d)).start()

    pass_on(0)
    pass_on(1)
    attend_late_fresh()
    for g in range(GROUPS):
        blend_group(g)
        project_group(g)

    for kind in range(2):
        for d in (to_next, 2):
            kv_copy(kind, 0, 2 * ((x + d) % NX) + zhi, z_peer).wait_recv()
        for d in others:
            kv_copy(kind, 0, 2 * ((x + d) % NX) + (zhi + 1) % 2, z_peer).wait_recv()
        for block in range(GROUP):
            fresh_pad[kind, pl.ds(slots + block * rows, rows), :] = kv_all[kind, block].astype(F32)
    start = p * slots - length
    begin = jnp.clip(start + slots, 0, 2 * slots)

    def place_rows(i, unused):
        at = pl.ds(pl.multiple_of(i * rows, rows), rows)
        token = start + i * rows + lax.broadcasted_iota(jnp.int32, (rows, HD), 0)
        written = jnp.logical_and(token >= 0, token < GROUP * rows)
        window = pl.ds(begin + i * rows, rows)
        for kind in range(2):
            cached = kraw[0, at, :] if kind == 0 else va[0, at, pl.ds(0, HD)]
            fresh = fresh_pad[kind, window, :].astype(BF16)
            updated[kind, at, :] = jnp.where(written, fresh, cached)
        return unused

    lax.fori_loop(0, GROUP, place_rows, 0)
    stores = [
        pltpu.make_async_copy(updated.at[0], keys_out, out_sem.at[0]),
        pltpu.make_async_copy(updated.at[1], values_out, out_sem.at[1]),
    ]
    for store in stores:
        store.start()

    for g in range(GROUPS):
        result = own_part[g]
        for d in (1, 3, 2):
            pr_copy(g, (NY - d) % NY).wait_recv()
        for d in (1, 2, 3):
            result = result + pr_in[g, d].astype(F32)
        out[pl.ds(g * (rows // GROUPS), rows // GROUPS), :] = result.astype(BF16)

    for k in range(3):
        ag_copy(k, h, s, sib, tok).wait_send()
    ag_copy(3, h, s, sib, tok).wait_send()
    for k in range(4, 7):
        ag_copy(k, h, s, sib).wait_send()
    for copy in wo_copies:
        copy.wait_send()
    for copy in pair_copies:
        copy.wait_send()
    for kind in range(2):
        for k in range(7):
            kv_copy(kind, k, p, z_peer).wait_send()
    for r in range(CHUNKS):
        for k in range(3):
            q_copy(k, 0, 0, r, 1, z_peer).wait_send()
        for copy in o_copies(0, r) + o_copies(1, r) + z_copies(r):
            copy.wait_send()
    for g in range(GROUPS):
        att_copy(g, c).wait_send()
        for d in (1, 2, 3):
            pr_copy(g, d).wait_send()
    for store in stores:
        store.wait()


def hand_on(*refs):
    sources, targets, held, (in_sem, out_sem) = refs[:3], refs[3:6], refs[6:9], refs[9:]
    pieces = []
    for at, source in enumerate(sources):
        share = source.shape[0] // 2
        pieces += [(at, half, pl.ds(half * share, share)) for half in range(2)]
    arriving = [
        pltpu.make_async_copy(sources[at].at[window], held[at].at[window], in_sem.at[at, half])
        for at, half, window in pieces
    ]
    leaving = [
        pltpu.make_async_copy(held[at].at[window], targets[at].at[window], out_sem.at[at, half])
        for at, half, window in pieces
    ]
    for copy in arriving:
        copy.start()
    for first, second in zip(arriving, leaving):
        first.wait()
        second.start()
    for copy in leaving:
        copy.wait()


def shards(
    tokens, norm_gain, w_query, w_key, w_value, w_out, keys_cache, values_cache,
    cached_lengths, rope_offsets,
):
    rows, width = tokens.shape
    slots = keys_cache.shape[0]
    heads = width // HD
    half = np.arange(HD) % (HD // 2)
    frequency = (ROPE_BASE ** (-half * 2.0 / HD)).astype(np.float32)[None]

    hbm_spec = pl.BlockSpec(memory_space=pltpu.HBM)
    vmem_spec = pl.BlockSpec(memory_space=pltpu.VMEM)
    smem_spec = pl.BlockSpec(memory_space=pltpu.SMEM)
    dma = pltpu.SemaphoreType.DMA
    block = (heads * rows // CHUNKS, HD)
    results = pl.pallas_call(
        kernel,
        out_shape=(
            jax.ShapeDtypeStruct((rows, width), BF16),
            jax.ShapeDtypeStruct((slots, HD), BF16),
            jax.ShapeDtypeStruct((slots, HD), BF16),
        ),
        in_specs=[hbm_spec] * 9 + [smem_spec] * 2,
        out_specs=(vmem_spec, hbm_spec, hbm_spec),
        scratch_shapes=[
            pltpu.VMEM((8, rows, width), BF16),
            pltpu.VMEM((8, 1, width), F32),
            pltpu.VMEM((1, HD), F32),
            pltpu.VMEM(w_query.shape, BF16),
            pltpu.VMEM(w_key.shape, BF16),
            pltpu.VMEM(w_value.shape, BF16),
            pltpu.VMEM((NY, 2 * width, width), BF16),
            pltpu.VMEM((2, slots, HD), BF16),
            pltpu.VMEM((2, 2 * HD, slots), BF16),
            pltpu.VMEM((2, slots, 2 * HD), BF16),
            pltpu.VMEM((2, HD, rows), BF16),
            pltpu.VMEM((2, rows, 2 * HD), BF16),
            pltpu.VMEM((rows, width + 2 * HD), F32),
            pltpu.VMEM((rows, HD), F32),
            pltpu.VMEM((rows, HD), F32),
            pltpu.VMEM((rows, HD), F32),
            pltpu.VMEM((2, 3 * slots, HD), F32),
            pltpu.VMEM((2, slots, HD), BF16),
            pltpu.VMEM((2, 2, CHUNKS) + block, BF16),
            pltpu.VMEM((2, GROUP, rows, HD), BF16),
            pltpu.VMEM((2, 2, CHUNKS) + block, BF16),
            pltpu.VMEM((2, 2, CHUNKS, 8, HD), F32),
            pltpu.VMEM((2, CHUNKS) + block, BF16),
            pltpu.VMEM((2, CHUNKS, 8, HD), F32),
            pltpu.VMEM((CHUNKS,) + block, BF16),
            pltpu.VMEM((CHUNKS, 8, HD), F32),
            pltpu.VMEM((CHUNKS,) + block, BF16),
            pltpu.VMEM((CHUNKS, 8, HD), F32),
            pltpu.VMEM((GROUPS, 2, rows // GROUPS, width), BF16),
            pltpu.VMEM((GROUPS, NY, rows // GROUPS, width), BF16),
            pltpu.VMEM((GROUPS, NY, rows // GROUPS, width), BF16),
            pltpu.VMEM((GROUPS, rows // GROUPS, width), F32),
            pltpu.VMEM((LATE_FRESH,) + block, BF16),
            pltpu.VMEM((LATE_FRESH, 8, HD), F32),
            dma((8,)), dma((NY,)), dma((7,)), dma((8,)), dma((NY,)), dma((NY,)), dma((2,)), dma((2,)),
            dma((3, CHUNKS)), dma((2, 2, CHUNKS)), dma((2, 7)), dma((2, GROUP)),
            dma((2, CHUNKS)), dma((2, CHUNKS)), dma((2, CHUNKS)), dma((2, CHUNKS)),
            dma((CHUNKS,)), dma((CHUNKS,)), dma((CHUNKS,)), dma((CHUNKS,)),
            dma((GROUPS,)), dma((GROUPS,)), dma((GROUPS, NY)), dma((GROUPS, NY)), dma((2,)),
        ],
        compiler_params=pltpu.CompilerParams(
            collective_id=0, has_side_effects=True, vmem_limit_bytes=64 << 20
        ),
        name="span_attention",
    )(
        tokens, norm_gain.reshape(8, 1, width), w_query, w_key, w_value, w_out,
        keys_cache, values_cache, frequency, cached_lengths, rope_offsets,
    )
    return pl.pallas_call(
        hand_on,
        out_shape=tuple(jax.ShapeDtypeStruct(one.shape, one.dtype) for one in results),
        in_specs=[hbm_spec] * 3,
        out_specs=(hbm_spec,) * 3,
        scratch_shapes=[pltpu.VMEM(one.shape, one.dtype) for one in results]
        + [dma((3, 2)), dma((3, 2))],
        name="hand_on",
    )(*results)


def solution(mesh):
    return jax.shard_map(
        shards,
        mesh=mesh,
        in_specs=(
            P("seq", "head"), P(), P(None, "head"), P(None, "head"), P(None, "head"),
            P("head", None), P("seq", "head"), P("seq", "head"), P(), P(),
        ),
        out_specs=(P("seq", "head"), P("seq", "head"), P("seq", "head")),
        check_vma=False,
    )
```

```python
import math

import jax
import jax.numpy as jnp
import numpy as np
from jax import lax
from jax.experimental import pallas as pl
from jax.experimental.pallas import tpu as pltpu
from jax.sharding import PartitionSpec as P

HD = 128
NX = 4
NZ = 8
NY = 4
GROUP = 8
NEG = -(2.0**100)
ROPE_BASE = 500000.0
EPS = 1e-05
LOG2E = 1.4426950408889634
F32 = jnp.float32
BF16 = jnp.bfloat16


def digit(number, place):
    value = number
    result = value % 10
    for at in range(1, 16):
        value = value // 10
        flag = (place + 16 - at) // 16 - (place + 15 - at) // 16
        result = result + flag * (value % 10 - number % 10)
    return result


def order_code(digits):
    return sum(d * 10**i for i, d in enumerate(digits))


ORDER = [(0, 0, 0), (0, 0, 1), (1, 0, 0), (1, 1, 0), (1, 1, 1), (1, 0, 1), (0, 1, 0), (0, 1, 1)]
LATE_FRESH = 2
STEP_FORWARD = (2, 3)
STEP_MERGE = (4, 5)
STEP_KEYS = 4
CHUNK = 2048
CHUNKS = 2
GROUPS = 2


def kernel(
    tok, gain, wq, wk, wv, wo, kc, vc, freq, lens, offs,
    out, keys_out, values_out,
    x_all, gain_v, freq_v, wq_v, wk_v, wv_v, wo_all, kraw, kT, va, kfT, vfa, acc, ssq,
    cos, sin, fresh_pad, updated, q_all, kv_all, o_buf, l_buf, o_in, l_in,
    oz_out, lz_out, oz_in, lz_in, att_all, pr_out, pr_in, own_part, late_o, late_l,
    load_sem, own_wo_sem, ag_send, ag_recv, wo_send, wo_recv, pair_send, pair_recv,
    q_send, q_recv, kv_send, kv_recv, o_send, o_recv, l_send, l_recv,
    z_send, z_recv, lz_send, lz_recv, att_send, att_recv, pr_send, pr_recv, out_sem,
):
    rows, width = tok.shape
    heads = width // HD
    slots = kc.shape[0]
    s = lax.axis_index("seq")
    h = lax.axis_index("head")
    x, z = s // NZ, s % NZ
    zhi = z // 4
    request = s % 4
    y, c = h // 2, h % 2
    p = s // 4
    z_peer = x * NZ + (z + 4) % NZ
    pz = z_peer // 4
    sib = y * 2 + (1 - c)
    odd = (x + c) % 2
    to_pair, to_next = 1 + 2 * odd, 3 - 2 * odd
    px = 2 * ((x + to_pair) % NX) + zhi
    part_rows = rows // CHUNKS

    def x_peer(d):
        return ((x + d) % NX) * NZ + z

    def y_peer(d):
        return ((y + d) % NY) * 2 + c

    def remote(src, dst, send, recv, seq, head):
        return pltpu.make_async_remote_copy(
            src_ref=src, dst_ref=dst, send_sem=send, recv_sem=recv,
            device_id=(seq, head), device_id_type=pl.DeviceIdType.MESH,
        )

    loads = [
        pltpu.make_async_copy(tok, x_all.at[h], load_sem.at[0]),
        pltpu.make_async_copy(wq, wq_v, load_sem.at[1]),
        pltpu.make_async_copy(wk, wk_v, load_sem.at[2]),
        pltpu.make_async_copy(wv, wv_v, load_sem.at[3]),
        pltpu.make_async_copy(kc, kraw.at[0], load_sem.at[4]),
        pltpu.make_async_copy(vc, va.at[0, :, pl.ds(0, HD)], load_sem.at[5]),
        pltpu.make_async_copy(gain, gain_v, load_sem.at[6]),
        pltpu.make_async_copy(freq, freq_v, load_sem.at[7]),
    ]
    loads[0].start()

    def wo_columns(yy, cc):
        return wo.at[:, pl.ds(pl.multiple_of((yy * 2 + cc) * width, width), width)]

    def wo_rows(yy, cc):
        return wo_all.at[yy, pl.ds(pl.multiple_of(cc * width, width), width), :]

    own_wo = [
        pltpu.make_async_copy(wo_columns(yy, c), wo_rows(yy, c), own_wo_sem.at[yy])
        for yy in range(NY)
    ]
    barrier = pltpu.get_barrier_semaphore()
    peers = [(z_peer, h), (s, y_peer(2)), (x_peer(2), h)]
    peers += [(s, y_peer(d)) for d in (1, 3)] + [(x_peer(d), h) for d in (1, 3)] + [(s, sib)]
    for seq, head in peers:
        pl.semaphore_signal(
            barrier, inc=1, device_id=(seq, head), device_id_type=pl.DeviceIdType.MESH
        )
    for kind in range(2):
        fresh_pad[kind, pl.ds(0, slots), :] = jnp.zeros((slots, HD), F32)
        fresh_pad[kind, pl.ds(2 * slots, slots), :] = jnp.zeros((slots, HD), F32)
    for side in range(2):
        va[side, :, pl.ds(HD, HD)] = jnp.ones((slots, HD), BF16)
        vfa[side, :, pl.ds(HD, HD)] = jnp.ones((rows, HD), BF16)
    acc[...] = jnp.zeros_like(acc)
    ssq[...] = jnp.zeros_like(ssq)
    l_buf[...] = jnp.zeros_like(l_buf)
    late_l[...] = jnp.zeros_like(late_l)
    pl.semaphore_wait(barrier, len(peers))

    def ag_copy(k, source, seq, head, src=None):
        return remote(
            x_all.at[source] if src is None else src, x_all.at[source],
            ag_send.at[k], ag_recv.at[source], seq, head,
        )

    for k, d in enumerate((2, 1, 3)):
        ag_copy(k, h, s, y_peer(d), tok).start()
    ag_copy(3, h, s, sib, tok).start()
    wo_copies = [
        remote(wo_columns(yy, 1 - c), wo_rows(yy, c), wo_send.at[yy], wo_recv.at[yy], s, sib)
        for yy in range(NY)
    ]
    pair_copies = [
        remote(kc, kraw.at[1], pair_send.at[0], pair_recv.at[0], x_peer(to_pair), h),
        remote(vc, va.at[1, :, pl.ds(0, HD)], pair_send.at[1], pair_recv.at[1], x_peer(to_pair), h),
    ]
    for copy in pair_copies:
        copy.start()
    for load in loads[1:] + own_wo:
        load.start()

    length = lens[request]

    def prepare_keys(side, holder):
        for at in range(0, slots, 512):
            kT[side, pl.ds(0, HD), pl.ds(at, 512)] = kraw[side, pl.ds(at, 512), :].T
        slot = holder * slots + lax.broadcasted_iota(jnp.int32, (HD, slots), 1)
        first_row = lax.broadcasted_iota(jnp.int32, (HD, slots), 0) == 0
        hidden = jnp.logical_and(first_row, slot >= length)
        kT[side, pl.ds(HD, HD), :] = jnp.where(hidden, NEG, 0.0).astype(BF16)

    loads[4].wait()
    loads[5].wait()
    prepare_keys(0, p)
    for at in (0, 1, 2, 3, 6, 7):
        loads[at].wait()
    place = offs[request] + length + p * rows
    place = place + lax.broadcasted_iota(jnp.int32, (rows, HD), 0)
    angles = place.astype(F32) * freq_v[...]
    sign = jnp.where(lax.broadcasted_iota(jnp.int32, (rows, HD), 1) < HD // 2, -1.0, 1.0)
    cos[...] = jnp.cos(angles)
    sin[...] = jnp.sin(angles) * sign

    def project(step, unused):
        d = digit(order_code([0, 0, 1, 3, 2, 1, 3, 2]), step)
        other = digit(order_code([0, 1, 0, 0, 0, 1, 1, 1]), step)
        source = ((y + d) % NY) * 2 + (c + other) % 2

        @pl.when(step > 0)
        def _():
            ag_copy(0, source, s, sib).wait_recv()

        @pl.when(jnp.logical_and(step >= 2, step < 5))
        def _():
            ag_copy(2 + step, source, s, sib).start()

        shard = x_all[source].astype(F32)
        square = shard * shard
        ssq[...] += square[:, :HD] + square[:, HD:2 * HD] + square[:, 2 * HD:]
        scaled = (shard * gain_v[source]).astype(BF16)
        at = pl.ds(pl.multiple_of(source * width, width), width)
        acc[:, pl.ds(0, width)] += jnp.dot(scaled, wq_v[at, :], preferred_element_type=F32)
        acc[:, pl.ds(width, HD)] += jnp.dot(scaled, wk_v[at, :], preferred_element_type=F32)
        acc[:, pl.ds(width + HD, HD)] += jnp.dot(scaled, wv_v[at, :], preferred_element_type=F32)
        return unused

    lax.fori_loop(0, 8, project, 0)

    scale = lax.rsqrt(jnp.sum(ssq[...], -1, keepdims=True) * (1.0 / (width * 8)) + EPS)
    cosine = cos[...]
    sine = sin[...]

    def rope(vectors):
        return vectors * cosine + pltpu.roll(vectors, HD // 2, 1) * sine

    def kv_copy(kind, k, block, seq):
        return remote(
            kv_all.at[kind, block], kv_all.at[kind, block],
            kv_send.at[kind, k], kv_recv.at[kind, block], seq, h,
        )

    def q_copy(k, dz, j, r, to_z, seq):
        return remote(
            q_all.at[dz, 0, r], q_all.at[to_z, j, r], q_send.at[k, r], q_recv.at[to_z, j, r], seq, h
        )

    fold = LOG2E / math.sqrt(HD)
    for r in range(CHUNKS):
        window = pl.ds(r * part_rows, part_rows)
        for hd in range(heads):
            vectors = acc[window, pl.ds(hd * HD, HD)] * scale[r * part_rows:(r + 1) * part_rows]
            turned = vectors * cos[window, :] + pltpu.roll(vectors, HD // 2, 1) * sin[window, :]
            q_all[0, 0, r, pl.ds(hd * part_rows, part_rows), :] = (turned * fold).astype(BF16)
        q_copy(0, 0, 0, r, 1, z_peer).start()
        q_copy(1, 0, 1, r, 0, x_peer(to_next)).start()
    fresh_key = rope(acc[:, pl.ds(width, HD)] * scale).astype(BF16)
    fresh_value = (acc[:, pl.ds(width + HD, HD)] * scale).astype(BF16)
    kv_all[0, p] = fresh_key
    kv_all[1, p] = fresh_value
    for kind in range(2):
        kv_copy(kind, 1, p, x_peer(to_pair)).start()
    for copy in wo_copies:
        copy.start()

    kfT[0] = fresh_key.T
    vfa[0, :, pl.ds(0, HD)] = fresh_value
    for copy in pair_copies:
        copy.wait_recv()
    prepare_keys(1, px)
    kfT[1] = jnp.zeros((HD, rows), BF16)
    vfa[1, :, pl.ds(0, HD)] = jnp.zeros((rows, HD), BF16)

    eye = lax.broadcasted_iota(jnp.int32, (part_rows, HD), 0) == lax.broadcasted_iota(
        jnp.int32, (part_rows, HD), 1
    )
    stacked = heads * part_rows
    first_lane = lax.broadcasted_iota(jnp.int32, (stacked, HD), 1) == 0
    one_lane = jnp.where(first_lane, 1.0, 0.0).astype(BF16)
    offset = lax.broadcasted_iota(jnp.int32, (stacked, rows), 0) % part_rows
    offset = offset - lax.broadcasted_iota(jnp.int32, (stacked, rows), 1)

    def o_copies(dz, r):
        return (
            remote(o_buf.at[dz, 1, r], o_in.at[dz, r], o_send.at[dz, r], o_recv.at[dz, r],
                   x_peer(to_next), h),
            remote(l_buf.at[dz, 1, r], l_in.at[dz, r], l_send.at[dz, r], l_recv.at[dz, r],
                   x_peer(to_next), h),
        )

    def z_copies(r):
        return (
            remote(oz_out.at[r], oz_in.at[r], z_send.at[r], z_recv.at[r], z_peer, h),
            remote(lz_out.at[r], lz_in.at[r], lz_send.at[r], lz_recv.at[r], z_peer, h),
        )

    def weigh(logsums):
        highest = logsums[0]
        for one in logsums[1:]:
            highest = jnp.maximum(highest, one)
        shares = [jnp.exp2(one - highest) for one in logsums]
        total = shares[0]
        for one in shares[1:]:
            total = total + one
        return [one / total for one in shares], highest + jnp.log(total) * LOG2E

    def blend(parts, shares, hd):
        result = None
        for part, share in zip(parts, shares):
            column = jnp.sum(jnp.where(eye, share[hd:hd + 1, :], 0.0), 1, keepdims=True)
            term = part[pl.ds(hd * part_rows, part_rows), :].astype(F32) * column
            result = term if result is None else result + term
        return result

    def merge_for_z(r):
        for copy in o_copies(1, r):
            copy.wait_recv()
        shares, merged = weigh([l_buf[1, 0, r], l_in[1, r]])
        lz_out[r] = merged
        for hd in range(heads):
            oz_out[r, pl.ds(hd * part_rows, part_rows), :] = blend(
                [o_buf.at[1, 0, r], o_in.at[1, r]], shares, hd
            ).astype(BF16)
        for copy in z_copies(r):
            copy.start()

    def att_copy(g, core):
        return remote(
            att_all.at[g, core], att_all.at[g, core], att_send.at[g], att_recv.at[g], s, sib
        )

    def pr_copy(g, d):
        back = (NY - d) % NY
        return remote(
            pr_out.at[g, d], pr_in.at[g, back], pr_send.at[g, d], pr_recv.at[g, back], s, y_peer(d)
        )

    def attend_late_fresh():
        for r in range(LATE_FRESH):
            scores = jnp.dot(q_all[0, 0, r], kfT[1], preferred_element_type=F32)
            scores = jnp.where(offset + r * part_rows + (p - px) * rows >= 0, scores, NEG)
            top = jnp.max(scores, -1, keepdims=True)
            weights = jnp.exp2(scores - top).astype(BF16)
            summed = jnp.dot(weights, vfa[1], preferred_element_type=F32)
            total = summed[:, HD:]
            late_o[r] = (summed[:, :HD] / total).astype(BF16)
            logsum = top + jnp.log(total) * LOG2E
            for hd in range(heads):
                late_l[r, pl.ds(hd, 1), :] = jnp.sum(
                    jnp.where(eye, logsum[hd * part_rows:(hd + 1) * part_rows], 0.0),
                    0, keepdims=True,
                )

    per_group = CHUNKS // GROUPS

    def blend_group(g):
        for k in range(per_group):
            r = g * per_group + k
            for copy in o_copies(0, r) + z_copies(r):
                copy.wait_recv()
            parts = [o_buf.at[0, 0, r], o_in.at[0, r], oz_in.at[r]]
            logsums = [l_buf[0, 0, r], l_in[0, r], lz_in[r]]
            if r < LATE_FRESH:
                parts.append(late_o.at[r])
                logsums.append(late_l[r])
            shares, merged = weigh(logsums)
            for hd in range(heads):
                att_all[g, c, pl.ds(k * part_rows, part_rows), pl.ds(hd * HD, HD)] = blend(
                    parts, shares, hd
                ).astype(BF16)
        att_copy(g, c).start()

    def project_group(g):
        if g == 0:
            for load in own_wo:
                load.wait()
            for copy in wo_copies:
                copy.wait_recv()
        att_copy(g, 1 - c).wait_recv()
        both = jnp.concatenate([att_all[g, 0], att_all[g, 1]], 1)
        for d in (2, 1, 3):
            part = jnp.dot(both, wo_all[(y + d) % NY], preferred_element_type=F32)
            pr_out[g, d] = part.astype(BF16)
            pr_copy(g, d).start()
        own_part[g] = jnp.dot(both, wo_all[y], preferred_element_type=F32)

    def attend(step, unused):
        dz = digit(order_code([o[0] for o in ORDER]), step)
        j = digit(order_code([o[1] for o in ORDER]), step)
        r = digit(order_code([o[2] for o in ORDER]), step)
        block = 2 * ((x + j * to_next) % NX) + (zhi + dz) % 2

        for chunk in range(CHUNKS):
            @pl.when(step == STEP_FORWARD[chunk])
            def _():
                q_copy(0, 0, 0, chunk, 1, z_peer).wait_recv()
                q_copy(2, 1, 1, chunk, 1, x_peer(to_next)).start()

        @pl.when(step == STEP_KEYS)
        def _():
            for kind in range(2):
                kv_copy(kind, 0, p, z_peer).start()

        @pl.when(step == LATE_FRESH)
        def _():
            for kind in range(2):
                kv_copy(kind, 1, px, z_peer).wait_recv()
            kfT[1] = kv_all[0, px].T
            vfa[1, :, pl.ds(0, HD)] = kv_all[1, px]

        @pl.when(j > 0)
        def _():
            q_copy(1, 0, 1, r, dz, z_peer).wait_recv()

        late = 1 - (step + len(ORDER) - LATE_FRESH) // len(ORDER)
        ahead = [
            offset + r * part_rows + (p_block - holder) * rows - far >= 0
            for p_block, holder, far in ((block, p, 0), (block, px, late * 2**20))
        ]

        query = q_all[dz, j, r]
        wide = jnp.concatenate([query, one_lane], 1)

        def score(side, at):
            scores = [jnp.dot(wide, kT[side, :, pl.ds(at, CHUNK)], preferred_element_type=F32)]
            if at + CHUNK == slots:
                fresh = jnp.dot(query, kfT[side], preferred_element_type=F32)
                scores.append(jnp.where(ahead[side], fresh, NEG))
            top = jnp.max(scores[0], -1, keepdims=True)
            for part in scores[1:]:
                top = jnp.maximum(top, jnp.max(part, -1, keepdims=True))
            return scores, top

        def weigh_values(side, at, scores, top):
            summed = None
            for part, value in zip(scores, (va[side, pl.ds(at, CHUNK), :], vfa[side])):
                weights = jnp.exp2(part - top).astype(BF16)
                term = jnp.dot(weights, value, preferred_element_type=F32)
                summed = term if summed is None else summed + term
            return summed, top

        pieces = [(side, at) for side in range(2) for at in range(0, slots, CHUNK)]
        current = score(*pieces[0])
        sums = []
        for number, piece in enumerate(pieces):
            following = score(*pieces[number + 1]) if number + 1 < len(pieces) else None
            sums.append(weigh_values(*piece, *current))
            current = following
        top = sums[0][1]
        for one, one_top in sums[1:]:
            top = jnp.maximum(top, one_top)
        summed = sums[0][0] * jnp.exp2(sums[0][1] - top)
        for one, one_top in sums[1:]:
            summed = summed + one * jnp.exp2(one_top - top)
        total = summed[:, HD:]
        o_buf[dz, j, r] = (summed[:, :HD] / total).astype(BF16)
        logsum = top + jnp.log(total) * LOG2E
        for hd in range(heads):
            l_buf[dz, j, r, pl.ds(hd, 1), :] = jnp.sum(
                jnp.where(eye, logsum[hd * part_rows:(hd + 1) * part_rows], 0.0), 0, keepdims=True
            )

        @pl.when(j > 0)
        def _():
            for copy in o_copies(dz, r):
                copy.start()

        for chunk in range(CHUNKS):
            @pl.when(step == STEP_MERGE[chunk])
            def _():
                merge_for_z(chunk)

        return unused

    lax.fori_loop(0, len(ORDER), attend, 0)

    others = (to_pair, to_next, 2)
    for kind in range(2):
        for k, d in ((2, to_next), (3, 2)):
            kv_copy(kind, k, p, x_peer(d)).start()

    def pass_on(kind):
        kv_copy(kind, 0, pz, z_peer).wait_recv()
        for k, d in enumerate(others):
            kv_copy(kind, 4 + k, pz, x_peer(d)).start()

    pass_on(0)
    pass_on(1)
    attend_late_fresh()
    for g in range(GROUPS):
        blend_group(g)
        project_group(g)

    for kind in range(2):
        for d in (to_next, 2):
            kv_copy(kind, 0, 2 * ((x + d) % NX) + zhi, z_peer).wait_recv()
        for d in others:
            kv_copy(kind, 0, 2 * ((x + d) % NX) + (zhi + 1) % 2, z_peer).wait_recv()
        for block in range(GROUP):
            fresh_pad[kind, pl.ds(slots + block * rows, rows), :] = kv_all[kind, block].astype(F32)
    start = p * slots - length
    begin = jnp.clip(start + slots, 0, 2 * slots)

    def place_rows(i, unused):
        at = pl.ds(pl.multiple_of(i * rows, rows), rows)
        token = start + i * rows + lax.broadcasted_iota(jnp.int32, (rows, HD), 0)
        written = jnp.logical_and(token >= 0, token < GROUP * rows)
        window = pl.ds(begin + i * rows, rows)
        for kind in range(2):
            cached = kraw[0, at, :] if kind == 0 else va[0, at, pl.ds(0, HD)]
            fresh = fresh_pad[kind, window, :].astype(BF16)
            updated[kind, at, :] = jnp.where(written, fresh, cached)
        return unused

    lax.fori_loop(0, GROUP, place_rows, 0)
    stores = [
        pltpu.make_async_copy(updated.at[0], keys_out, out_sem.at[0]),
        pltpu.make_async_copy(updated.at[1], values_out, out_sem.at[1]),
    ]
    for store in stores:
        store.start()

    for g in range(GROUPS):
        result = own_part[g]
        for d in (1, 3, 2):
            pr_copy(g, (NY - d) % NY).wait_recv()
        for d in (1, 2, 3):
            result = result + pr_in[g, d].astype(F32)
        out[pl.ds(g * (rows // GROUPS), rows // GROUPS), :] = result.astype(BF16)

    for k in range(3):
        ag_copy(k, h, s, sib, tok).wait_send()
    ag_copy(3, h, s, sib, tok).wait_send()
    for k in range(4, 7):
        ag_copy(k, h, s, sib).wait_send()
    for copy in wo_copies:
        copy.wait_send()
    for copy in pair_copies:
        copy.wait_send()
    for kind in range(2):
        for k in range(7):
            kv_copy(kind, k, p, z_peer).wait_send()
    for r in range(CHUNKS):
        for k in range(3):
            q_copy(k, 0, 0, r, 1, z_peer).wait_send()
        for copy in o_copies(0, r) + o_copies(1, r) + z_copies(r):
            copy.wait_send()
    for g in range(GROUPS):
        att_copy(g, c).wait_send()
        for d in (1, 2, 3):
            pr_copy(g, d).wait_send()
    for store in stores:
        store.wait()


def hand_on(*refs):
    sources, targets, held, (in_sem, out_sem) = refs[:3], refs[3:6], refs[6:9], refs[9:]
    pieces = []
    for at, source in enumerate(sources):
        share = source.shape[0] // 2
        pieces += [(at, half, pl.ds(half * share, share)) for half in range(2)]
    arriving = [
        pltpu.make_async_copy(sources[at].at[window], held[at].at[window], in_sem.at[at, half])
        for at, half, window in pieces
    ]
    leaving = [
        pltpu.make_async_copy(held[at].at[window], targets[at].at[window], out_sem.at[at, half])
        for at, half, window in pieces
    ]
    for copy in arriving:
        copy.start()
    for first, second in zip(arriving, leaving):
        first.wait()
        second.start()
    for copy in leaving:
        copy.wait()


def shards(
    tokens, norm_gain, w_query, w_key, w_value, w_out, keys_cache, values_cache,
    cached_lengths, rope_offsets,
):
    rows, width = tokens.shape
    slots = keys_cache.shape[0]
    heads = width // HD
    half = np.arange(HD) % (HD // 2)
    frequency = (ROPE_BASE ** (-half * 2.0 / HD)).astype(np.float32)[None]

    hbm_spec = pl.BlockSpec(memory_space=pltpu.HBM)
    vmem_spec = pl.BlockSpec(memory_space=pltpu.VMEM)
    smem_spec = pl.BlockSpec(memory_space=pltpu.SMEM)
    dma = pltpu.SemaphoreType.DMA
    block = (heads * rows // CHUNKS, HD)
    results = pl.pallas_call(
        kernel,
        out_shape=(
            jax.ShapeDtypeStruct((rows, width), BF16),
            jax.ShapeDtypeStruct((slots, HD), BF16),
            jax.ShapeDtypeStruct((slots, HD), BF16),
        ),
        in_specs=[hbm_spec] * 9 + [smem_spec] * 2,
        out_specs=(vmem_spec, hbm_spec, hbm_spec),
        scratch_shapes=[
            pltpu.VMEM((8, rows, width), BF16),
            pltpu.VMEM((8, 1, width), F32),
            pltpu.VMEM((1, HD), F32),
            pltpu.VMEM(w_query.shape, BF16),
            pltpu.VMEM(w_key.shape, BF16),
            pltpu.VMEM(w_value.shape, BF16),
            pltpu.VMEM((NY, 2 * width, width), BF16),
            pltpu.VMEM((2, slots, HD), BF16),
            pltpu.VMEM((2, 2 * HD, slots), BF16),
            pltpu.VMEM((2, slots, 2 * HD), BF16),
            pltpu.VMEM((2, HD, rows), BF16),
            pltpu.VMEM((2, rows, 2 * HD), BF16),
            pltpu.VMEM((rows, width + 2 * HD), F32),
            pltpu.VMEM((rows, HD), F32),
            pltpu.VMEM((rows, HD), F32),
            pltpu.VMEM((rows, HD), F32),
            pltpu.VMEM((2, 3 * slots, HD), F32),
            pltpu.VMEM((2, slots, HD), BF16),
            pltpu.VMEM((2, 2, CHUNKS) + block, BF16),
            pltpu.VMEM((2, GROUP, rows, HD), BF16),
            pltpu.VMEM((2, 2, CHUNKS) + block, BF16),
            pltpu.VMEM((2, 2, CHUNKS, 8, HD), F32),
            pltpu.VMEM((2, CHUNKS) + block, BF16),
            pltpu.VMEM((2, CHUNKS, 8, HD), F32),
            pltpu.VMEM((CHUNKS,) + block, BF16),
            pltpu.VMEM((CHUNKS, 8, HD), F32),
            pltpu.VMEM((CHUNKS,) + block, BF16),
            pltpu.VMEM((CHUNKS, 8, HD), F32),
            pltpu.VMEM((GROUPS, 2, rows // GROUPS, width), BF16),
            pltpu.VMEM((GROUPS, NY, rows // GROUPS, width), BF16),
            pltpu.VMEM((GROUPS, NY, rows // GROUPS, width), BF16),
            pltpu.VMEM((GROUPS, rows // GROUPS, width), F32),
            pltpu.VMEM((LATE_FRESH,) + block, BF16),
            pltpu.VMEM((LATE_FRESH, 8, HD), F32),
            dma((8,)), dma((NY,)), dma((7,)), dma((8,)), dma((NY,)), dma((NY,)), dma((2,)), dma((2,)),
            dma((3, CHUNKS)), dma((2, 2, CHUNKS)), dma((2, 7)), dma((2, GROUP)),
            dma((2, CHUNKS)), dma((2, CHUNKS)), dma((2, CHUNKS)), dma((2, CHUNKS)),
            dma((CHUNKS,)), dma((CHUNKS,)), dma((CHUNKS,)), dma((CHUNKS,)),
            dma((GROUPS,)), dma((GROUPS,)), dma((GROUPS, NY)), dma((GROUPS, NY)), dma((2,)),
        ],
        compiler_params=pltpu.CompilerParams(
            collective_id=0, has_side_effects=True, vmem_limit_bytes=64 << 20
        ),
        name="span_attention",
    )(
        tokens, norm_gain.reshape(8, 1, width), w_query, w_key, w_value, w_out,
        keys_cache, values_cache, frequency, cached_lengths, rope_offsets,
    )
    return pl.pallas_call(
        hand_on,
        out_shape=tuple(jax.ShapeDtypeStruct(one.shape, one.dtype) for one in results),
        in_specs=[hbm_spec] * 3,
        out_specs=(hbm_spec,) * 3,
        scratch_shapes=[pltpu.VMEM(one.shape, one.dtype) for one in results]
        + [dma((3, 2)), dma((3, 2))],
        name="hand_on",
    )(*results)


def solution(mesh):
    return jax.shard_map(
        shards,
        mesh=mesh,
        in_specs=(
            P("seq", "head"), P(), P(None, "head"), P(None, "head"), P(None, "head"),
            P("head", None), P("seq", "head"), P("seq", "head"), P(), P(),
        ),
        out_specs=(P("seq", "head"), P("seq", "head"), P("seq", "head")),
        check_vma=False,
    )
```
